32 devices in a mesh: ctx: 8 (over z, y), shard: 4 (over x, core).
Axes of the slice: x: 2, y: 2, z: 4, core: 2. Of those that a mesh axis runs over, the one named last changes fastest.
Arguments:
- layer_input: bfloat16 [4096, 768], P(('ctx', 'shard')), may hold values from -6 to 6
- norm1_gain: bfloat16 [768], P('shard'), may hold values from 0.5 to 1.5
- qkv_weight: bfloat16 [3, 768, 768], P(None, None, 'shard'), may hold values from -0.21875 to 0.21875
- rel_bias: float32 [32, 12], P(None, 'shard'), may hold values from -4 to 300
- out_weight: bfloat16 [768, 768], P('shard'), may hold values from -1.5 to 1.5
- norm2_gain: bfloat16 [768], P('shard'), may hold values from 0.5 to 1.5
- router_weight: bfloat16 [768, 16], P('shard'), may hold values from -0.21875 to 0.21875
- expert_up: bfloat16 [16, 768, 3072], P('ctx', None, 'shard'), may hold values from -0.21875 to 0.21875
- expert_down: bfloat16 [16, 3072, 768], P('ctx', 'shard'), may hold values from -0.109375 to 0.109375
- routes: int32 [4096, 2], P(('ctx', 'shard')), may hold values from 0 to 15, all different within a row; in each aligned block of 128 rows (0 to 127, 128 to 255, ...) at most 32 rows name the same one
- cotangent: bfloat16 [4096, 768], P(('ctx', 'shard')), may hold values from -6 to 6
Outputs:
- output: float32 [4096, 768], P(('ctx', 'shard'))
- input_gradient: float32 [4096, 768], P(('ctx', 'shard'))
- gradient_norm1_gain: float32 [768], P('shard')
- grad_qkv_weight: float32 [3, 768, 768], P(None, None, 'shard')
- grad_rel_bias: float32 [32, 12], P(None, 'shard')
- grad_out_weight: float32 [768, 768], P('shard')
- gradient_norm2_gain: float32 [768], P('shard')
- grad_router_weight: float32 [768, 16], P('shard')
- grad_expert_up: float32 [16, 768, 3072], P('ctx', None, 'shard')
- grad_expert_down: float32 [16, 3072, 768], P('ctx', 'shard')
The draws below stay inside these ranges and needn't reach their ends.
Inputs may be any that keep to these rules, and one draw needn't show every extreme that they name: `routes`: A token's two experts differ. Among the rows of one device no expert is named more than 32 times, and in some device an expert is named exactly 32 times.
All inputs are finite; a program needn't handle non-finite values.
Results may differ from the reference program's by a relative error of at most 0.025.
Values may be sent and summed in bfloat16 or wider, within the bound.
No kernel may reach another device: no remote copies, remote signals or barrier semaphores. Data moves between devices by JAX's collectives and lax.ppermute only.
A program may use at most 192 MiB of HBM per device.

```python
import math
import jax
import jax.numpy as jnp
import numpy as np
from jax import lax

D = 768
H = 12
HD = 64
FF = 3072
BUCKETS = 32
TOK_DEV = 128
E = 16
CAP = 32
HALF = 256
TOKENS = 4096


def draw_rel_bias(key, part):
    base_key = jax.random.fold_in(jax.random.fold_in(key, 11), 0)
    bias_table = jnp.clip(jax.random.normal(base_key, (BUCKETS, H), jnp.float32), -4.0, 4.0)
    return bias_table


def block_scale(stream_key, extent, pieces, low, high):
    loudness = 1.0
    for axis_at, blocks in pieces:
        steps = jax.random.uniform(jax.random.fold_in(jax.random.fold_in(stream_key, 6), axis_at), (blocks,), jnp.float32, low / len(pieces), high / len(pieces))
        loudness = loudness * jnp.repeat(jnp.exp(steps), extent[axis_at] // blocks).reshape((-1,) + (1,) * (len(extent) - 1 - axis_at))
    return loudness


def deal_out(rng, own, number, rows, number_of, top, limit, lean):
    ranking = jax.random.permutation(rng, number_of)
    crowded, usual = portions_of(number_of, rows * top, limit, lean, True), portions_of(number_of, rows * top, limit, lean, False)
    places = jnp.arange(number_of)

    def named(lengths, offset_by):
        used = int((lengths > 0).sum())
        fixed = max(1, used // 4)
        shifted = fixed + (places - fixed + offset_by * (used - fixed)) % max(1, number_of - fixed)
        return jnp.zeros((number_of,), jnp.int32).at[ranking[jnp.where(places < fixed, places, shifted)]].set(jnp.asarray(lengths, jnp.int32))

    lengths = jnp.where(number % 4 == 0, named(crowded, number // 4), named(usual, number - number // 4 - 1))
    mixed = jax.random.permutation(jax.random.fold_in(own, 3), number_of)
    giver, receiver = mixed[0:number_of // 2 * 2:2], mixed[1:number_of // 2 * 2:2]
    margin = jnp.minimum(lengths[giver] - 1, limit - lengths[receiver]) // 2
    margin = jnp.where((giver == ranking[0]) | (receiver == ranking[0]) | (lengths[receiver] == 0), 0, jnp.maximum(margin, 0))
    shifted = jax.random.randint(jax.random.fold_in(own, 4), (number_of // 2,), 0, 1 << 20) % (margin + 1)
    lengths = lengths.at[giver].add(-shifted).at[receiver].add(shifted)
    items = jnp.searchsorted(jnp.cumsum(lengths), jnp.arange(rows * top), side="right").astype(jnp.int32)
    listing = items.reshape(top, rows).T
    listing = listing[jax.random.permutation(jax.random.fold_in(own, 1), rows)]
    offset_by = jax.random.randint(jax.random.fold_in(own, 2), (rows, 1), 0, top)
    return jnp.take_along_axis(listing, (jnp.arange(top)[None, :] + offset_by) % top, axis=1)


def portions_of(amount, total, most, lean, full):
    loads = [(1 << 20) // math.isqrt(standing ** lean) + 1 for standing in range(1, amount + 1)]
    largest = most if full else min(most, max(-(-total // amount), total * loads[0] // sum(loads)))
    least = 1 if total - largest >= amount - 1 else 0
    given, rest = [largest] + [least] * (amount - 1), total - largest - least * (amount - 1)
    while rest > 0:
        movable = [i for i in range(1, amount) if given[i] < largest] or [i for i in range(1, amount) if given[i] < most]
        mass, budget = sum([loads[i] for i in movable]), rest
        for i in movable:
            addition = min(most - given[i], max(1, budget * loads[i] // mass), rest)
            given[i] = given[i] + addition
            rest = rest - addition
    return np.array(given)


def normal_values(rng, dims, scale, reach, pieces=(), kind=jnp.bfloat16):
    level = block_scale(rng, dims, pieces, -0.22, 0.18) if pieces else 1.0
    drawn = jax.random.normal(rng, dims, jnp.float32) * scale * level
    return jnp.minimum(jnp.maximum(drawn, -reach), reach).astype(kind)


def setup_inputs(seed: int = 0) -> dict:
    seeds = jax.random.split(jax.random.key(seed), 12)
    layer_input = normal_values(seeds[0], (TOKENS, D), 1.0, 6.0, ((0, 32),))
    norm1_gain = jnp.clip(1.0 + 0.1 * jax.random.normal(seeds[1], (D,), jnp.float32), 0.5, 1.5).astype(jnp.bfloat16)
    qkv_weight = normal_values(seeds[2], (3, D, D), D ** -0.5, 0.21875, ((2, 4),))
    rel_bias = draw_rel_bias(jax.random.fold_in(seeds[11], 71), 0)
    out_weight = normal_values(seeds[4], (D, D), (HD // 4) ** -0.5, 1.5, ((0, 4),))
    norm2_gain = jnp.clip(1.0 + 0.1 * jax.random.normal(seeds[5], (D,), jnp.float32), 0.5, 1.5).astype(jnp.bfloat16)
    router_weight = normal_values(seeds[6], (D, E), D ** -0.5, 0.21875, ((0, 4),))
    expert_up = normal_values(seeds[7], (E, D, FF), D ** -0.5, 0.21875, ((0, 8), (2, 4)))
    expert_down = normal_values(seeds[8], (E, FF, D), FF ** -0.5, 0.109375, ((0, 8), (1, 4)))
    routes_keys = jax.random.split(jax.random.fold_in(seeds[9], 1), TOKENS // TOK_DEV)
    routes_turns = jax.random.permutation(jax.random.fold_in(seeds[9], 3), TOKENS // TOK_DEV)
    routes = jax.vmap(lambda own, number: deal_out(jax.random.fold_in(seeds[9], 2), own, number, TOK_DEV, E, 2, CAP, 2))(routes_keys, routes_turns).reshape((TOKENS, 2))
    cotangent = normal_values(seeds[10], (TOKENS, D), 1.0, 6.0, ((0, 32),))
    return dict(layer_input=layer_input, norm1_gain=norm1_gain, qkv_weight=qkv_weight, rel_bias=rel_bias, out_weight=out_weight, norm2_gain=norm2_gain, router_weight=router_weight, expert_up=expert_up, expert_down=expert_down, routes=routes, cotangent=cotangent)


NORM_EPS = 1e-06
MASKED = -1e+30
HIGHEST = lax.Precision.HIGHEST

def bucket_of(distance):
    clipped = jnp.maximum(distance, 0)
    square = clipped * clipped
    counted = jnp.zeros_like(clipped)
    for exponent in range(1, 16):
        counted = counted + (square >= 256 << exponent).astype(jnp.int32)
    return jnp.where(clipped < 16, clipped, 16 + counted)

def block_ids(group_index, groups):
    return jnp.stack([group_index, 2 * groups - 1 - group_index]).astype(jnp.int32)

def positions(group_index, groups, half_rows):
    starts = block_ids(group_index, groups) * half_rows
    return (starts[:, None] + jnp.arange(half_rows, dtype=jnp.int32)[None, :]).reshape(-1)

def tile_bias(deltas, bias_table, tile_rows):
    offsets = jnp.arange(2 * tile_rows - 1, dtype=jnp.int32)
    distance = deltas[:, :, None] + (tile_rows - 1) - offsets[None, None, :]
    onehot = (bucket_of(distance)[..., None] == jnp.arange(bias_table.shape[0], dtype=jnp.int32)).astype(bias_table.dtype)
    values = jnp.einsum('abtk,kh->abht', onehot, bias_table, precision=HIGHEST)
    query_tiles, key_tiles, head_count = (values.shape[0], values.shape[1], values.shape[2])
    padded = jnp.pad(values, ((0, 0), (0, 0), (0, 0), (0, 1)))
    broadcasted = jnp.broadcast_to(padded[:, :, :, None, :], (query_tiles, key_tiles, head_count, tile_rows, 2 * tile_rows))
    flattened = broadcasted.reshape(query_tiles, key_tiles, head_count, 2 * tile_rows * tile_rows)
    flattened = flattened[..., :tile_rows * (2 * tile_rows - 1)]
    skewed = flattened.reshape(query_tiles, key_tiles, head_count, tile_rows, 2 * tile_rows - 1)[..., tile_rows - 1:]
    bias_tile = skewed.transpose(2, 0, 3, 1, 4).reshape(head_count, query_tiles * tile_rows, key_tiles * tile_rows)
    return (bias_tile, onehot)

def bias_grad(grad_scores, onehot, tile_rows):
    head_count = grad_scores.shape[0]
    query_tiles = grad_scores.shape[1] // tile_rows
    key_tiles = grad_scores.shape[2] // tile_rows
    tile_blocks = grad_scores.reshape(head_count, query_tiles, tile_rows, key_tiles, tile_rows).transpose(1, 3, 0, 2, 4)
    flipped = tile_blocks[:, :, :, ::-1, :]
    padded = jnp.pad(flipped, ((0, 0), (0, 0), (0, 0), (0, 0), (0, tile_rows)))
    flattened = padded.reshape(query_tiles, key_tiles, head_count, 2 * tile_rows * tile_rows)
    flattened = flattened[..., :tile_rows * (2 * tile_rows - 1)]
    sheared = flattened.reshape(query_tiles, key_tiles, head_count, tile_rows, 2 * tile_rows - 1)
    diagonal = lax.optimization_barrier(jnp.sum(sheared, axis=3))
    return jnp.einsum('abht,abtk->kh', diagonal, onehot, precision=HIGHEST)

def rounded(values):
    return lax.optimization_barrier(values.astype(jnp.bfloat16)).astype(jnp.float32)

def gelu_tanh(values):
    return jax.nn.gelu(values, approximate=True)

def ref_scores(queries, keys, bias_table, query_group, key_group, groups):
    deltas = (block_ids(query_group, groups)[:, None] - block_ids(key_group, groups)[None, :]) * HALF
    bias_tile, onehot = tile_bias(deltas, bias_table, HALF)
    scores = jnp.einsum('qhd,khd->hqk', queries.astype(jnp.float32), keys.astype(jnp.float32), precision=HIGHEST)
    scores = scores * HD ** (-0.5) + bias_tile
    causal = positions(query_group, groups, HALF)[:, None] >= positions(key_group, groups, HALF)[None, :]
    return (jnp.where(causal, scores, MASKED), causal, onehot)

def reference(layer_input, norm1_gain, qkv_weight, rel_bias, out_weight, norm2_gain, router_weight, expert_up, expert_down, routes, cotangent):
    groups = TOKENS // (2 * HALF)
    group_rows = 2 * HALF
    devices = TOKENS // TOK_DEV
    group_ids = jnp.arange(groups, dtype=jnp.int32)
    bias_table = rel_bias.astype(jnp.float32)
    input_single_float = layer_input.astype(jnp.float32)
    first_inverse_norm = lax.rsqrt(lax.optimization_barrier(jnp.mean(input_single_float * input_single_float, axis=-1, keepdims=True)) + NORM_EPS)
    first_unit_rows = input_single_float * first_inverse_norm
    first_norm_gain = norm1_gain.astype(jnp.float32)
    first_normed_rows = (first_unit_rows * first_norm_gain).astype(jnp.bfloat16)
    queries = jnp.dot(first_normed_rows, qkv_weight[0], preferred_element_type=jnp.float32).astype(jnp.bfloat16)
    keys_all = jnp.dot(first_normed_rows, qkv_weight[1], preferred_element_type=jnp.float32).astype(jnp.bfloat16)
    values_all = jnp.dot(first_normed_rows, qkv_weight[2], preferred_element_type=jnp.float32).astype(jnp.bfloat16)
    head_shape = (groups, group_rows, H, HD)
    query_heads = queries.reshape(head_shape)
    key_heads = keys_all.reshape(head_shape)
    value_heads = values_all.reshape(head_shape)

    def forward_group(query_group):
        query_block = query_heads[query_group]

        def advance(carried, key_group):
            running_max, denominator, accumulated = carried
            scores, causal, onehot = ref_scores(query_block, key_heads[key_group], bias_table, query_group, key_group, groups)
            new_max = jnp.maximum(running_max, lax.optimization_barrier(jnp.max(scores, axis=-1)))
            factor = jnp.exp(running_max - new_max)
            weights = jnp.where(causal, jnp.exp(scores - new_max[..., None]), 0.0)
            denominator = denominator * factor + lax.optimization_barrier(jnp.sum(weights, axis=-1))
            product = jnp.einsum('hqk,khd->hqd', rounded(weights), value_heads[key_group].astype(jnp.float32), precision=HIGHEST)
            accumulated = accumulated * factor[..., None] + product
            return ((new_max, denominator, accumulated), None)
        start_state = (jnp.full((H, group_rows), MASKED, jnp.float32), jnp.zeros((H, group_rows), jnp.float32), jnp.zeros((H, group_rows, HD), jnp.float32))
        (running_max, denominator, accumulated), _ = lax.scan(advance, start_state, group_ids)
        return ((accumulated / denominator[..., None]).transpose(1, 0, 2), running_max + jnp.log(denominator))
    heads_out, log_sums = lax.map(forward_group, group_ids)
    attn_heads = heads_out.reshape(TOKENS, D).astype(jnp.bfloat16)
    hidden_state = input_single_float + jnp.dot(attn_heads, out_weight, preferred_element_type=jnp.float32)
    second_inverse_norm = lax.rsqrt(lax.optimization_barrier(jnp.mean(hidden_state * hidden_state, axis=-1, keepdims=True)) + NORM_EPS)
    second_unit_rows = hidden_state * second_inverse_norm
    second_norm_gain = norm2_gain.astype(jnp.float32)
    second_normed_rows = (second_unit_rows * second_norm_gain).astype(jnp.bfloat16)
    probabilities = jax.nn.softmax(jnp.dot(second_normed_rows, router_weight, preferred_element_type=jnp.float32), axis=-1)
    gates = jnp.take_along_axis(probabilities, routes, axis=1)
    flat_routes = routes.reshape(devices, 2 * TOK_DEV)
    hits = (flat_routes[..., None] == jnp.arange(E, dtype=jnp.int32)).astype(jnp.int32)
    slots = lax.optimization_barrier(jnp.sum((jnp.cumsum(hits, axis=1) - hits) * hits, axis=-1)).astype(jnp.int32)
    device_ids = jnp.broadcast_to(jnp.arange(devices, dtype=jnp.int32)[:, None], flat_routes.shape)

    def to_slots(token_rows):
        buffer = jnp.zeros((E, devices, CAP, D), jnp.bfloat16)
        filled = buffer.at[flat_routes, device_ids, slots].set(token_rows.reshape(devices, 2 * TOK_DEV, D))
        return filled.reshape(E, devices * CAP, D)

    def from_slots(buffer):
        return buffer.reshape(E, devices, CAP, D)[flat_routes, device_ids, slots].reshape(TOKENS, 2, D)
    expert_in = to_slots(jnp.repeat(second_normed_rows, 2, axis=0))

    def expert_forward(operands):
        slot_rows, first_weight, second_weight = operands
        activation = gelu_tanh(jnp.dot(slot_rows, first_weight, preferred_element_type=jnp.float32)).astype(jnp.bfloat16)
        return jnp.dot(activation, second_weight, preferred_element_type=jnp.float32).astype(jnp.bfloat16)
    expert_rows = from_slots(lax.map(expert_forward, (expert_in, expert_up, expert_down)))
    output = hidden_state + lax.optimization_barrier(jnp.sum(gates[..., None] * expert_rows.astype(jnp.float32), axis=1))
    upstream_gradient = cotangent.astype(jnp.float32)
    grad_gate = lax.optimization_barrier(jnp.sum(upstream_gradient[:, None, :] * expert_rows.astype(jnp.float32), axis=-1))
    grad_rows = (gates[..., None] * upstream_gradient[:, None, :]).astype(jnp.bfloat16)
    grad_slots = to_slots(grad_rows.reshape(2 * TOKENS, D))

    def expert_backward(operands):
        slot_rows, slot_grads, first_weight, second_weight = operands
        inner = jnp.dot(slot_rows, first_weight, preferred_element_type=jnp.float32)
        act_float, act_vjp = jax.vjp(gelu_tanh, inner)
        activation = act_float.astype(jnp.bfloat16)
        grad_second = jnp.dot(activation.T, slot_grads, preferred_element_type=jnp.float32)
        grad_act = jnp.dot(slot_grads, second_weight.T, preferred_element_type=jnp.float32)
        grad_inner = act_vjp(grad_act)[0].astype(jnp.bfloat16)
        grad_first = jnp.dot(slot_rows.T, grad_inner, preferred_element_type=jnp.float32)
        grad_back = jnp.dot(grad_inner, first_weight.T, preferred_element_type=jnp.float32).astype(jnp.bfloat16)
        return (grad_first, grad_second, grad_back)
    grad_expert_up, grad_expert_down, grad_back = lax.map(expert_backward, (expert_in, grad_slots, expert_up, expert_down))
    grad_from_experts = lax.optimization_barrier(jnp.sum(from_slots(grad_back).astype(jnp.float32), axis=1))
    chosen = (routes[..., None] == jnp.arange(E, dtype=jnp.int32)).astype(jnp.float32)
    grad_probs = lax.optimization_barrier(jnp.sum(chosen * grad_gate[..., None], axis=1))
    grad_logits = probabilities * (grad_probs - lax.optimization_barrier(jnp.sum(probabilities * grad_probs, axis=-1, keepdims=True)))
    grad_logits = grad_logits.astype(jnp.bfloat16)
    grad_router_weight = jnp.dot(second_normed_rows.T, grad_logits, preferred_element_type=jnp.float32)
    second_normed_gradient = jnp.dot(grad_logits, router_weight.T, preferred_element_type=jnp.float32) + grad_from_experts
    gradient_norm2_gain = lax.optimization_barrier(jnp.sum(second_normed_gradient * second_unit_rows, axis=0))
    second_scaled_rows = second_norm_gain * second_normed_gradient
    hidden_gradient = upstream_gradient + second_inverse_norm * (second_scaled_rows - second_unit_rows * lax.optimization_barrier(jnp.mean(second_scaled_rows * second_unit_rows, axis=-1, keepdims=True)))
    hidden_grad_b = hidden_gradient.astype(jnp.bfloat16)
    grad_out_weight = jnp.dot(attn_heads.T, hidden_grad_b, preferred_element_type=jnp.float32)
    grad_heads = jnp.dot(hidden_grad_b, out_weight.T, preferred_element_type=jnp.float32).astype(jnp.bfloat16)
    delta_rows = lax.optimization_barrier(jnp.sum((grad_heads.astype(jnp.float32) * attn_heads.astype(jnp.float32)).reshape(TOKENS, H, HD), axis=-1))
    delta_groups = delta_rows.reshape(groups, group_rows, H).transpose(0, 2, 1)
    grad_head_blocks = grad_heads.reshape(head_shape)

    def query_side(query_group):
        query_block = query_heads[query_group]
        grad_block = grad_head_blocks[query_group]
        lse_block = log_sums[query_group]
        delta_block = delta_groups[query_group]

        def advance(carried, key_group):
            grad_query, grad_table = carried
            scores, causal, onehot = ref_scores(query_block, key_heads[key_group], bias_table, query_group, key_group, groups)
            probs_att = jnp.where(causal, jnp.exp(scores - lse_block[..., None]), 0.0)
            grad_probs_att = jnp.einsum('qhd,khd->hqk', grad_block.astype(jnp.float32), value_heads[key_group].astype(jnp.float32), precision=HIGHEST)
            grad_scores = probs_att * (grad_probs_att - delta_block[..., None])
            grad_query = grad_query + jnp.einsum('hqk,khd->qhd', rounded(grad_scores), key_heads[key_group].astype(jnp.float32), precision=HIGHEST)
            grad_table = grad_table + bias_grad(grad_scores, onehot, HALF)
            return ((grad_query, grad_table), None)
        start_state = (jnp.zeros((group_rows, H, HD), jnp.float32), jnp.zeros((BUCKETS, H), jnp.float32))
        (grad_query, grad_table), _ = lax.scan(advance, start_state, group_ids)
        return (grad_query * HD ** (-0.5), grad_table)
    grad_queries, grad_tables = lax.map(query_side, group_ids)
    grad_rel_bias = lax.optimization_barrier(jnp.sum(grad_tables, axis=0))

    def key_side(key_group):
        key_block = key_heads[key_group]
        value_block = value_heads[key_group]

        def advance(carried, query_group):
            grad_key, grad_value = carried
            scores, causal, onehot = ref_scores(query_heads[query_group], key_block, bias_table, query_group, key_group, groups)
            probs_att = jnp.where(causal, jnp.exp(scores - log_sums[query_group][..., None]), 0.0)
            grad_block = grad_head_blocks[query_group].astype(jnp.float32)
            grad_value = grad_value + jnp.einsum('hqk,qhd->khd', rounded(probs_att), grad_block, precision=HIGHEST)
            grad_probs_att = jnp.einsum('qhd,khd->hqk', grad_block, value_block.astype(jnp.float32), precision=HIGHEST)
            grad_scores = probs_att * (grad_probs_att - delta_groups[query_group][..., None])
            grad_key = grad_key + jnp.einsum('hqk,qhd->khd', rounded(grad_scores), query_heads[query_group].astype(jnp.float32), precision=HIGHEST)
            return ((grad_key, grad_value), None)
        start_state = (jnp.zeros((group_rows, H, HD), jnp.float32), jnp.zeros((group_rows, H, HD), jnp.float32))
        (grad_key, grad_value), _ = lax.scan(advance, start_state, group_ids)
        return (grad_key * HD ** (-0.5), grad_value)
    grad_keys, grad_values = lax.map(key_side, group_ids)
    grad_q = grad_queries.reshape(TOKENS, D).astype(jnp.bfloat16)
    grad_k = grad_keys.reshape(TOKENS, D).astype(jnp.bfloat16)
    grad_v = grad_values.reshape(TOKENS, D).astype(jnp.bfloat16)
    grad_qkv_weight = jnp.stack([jnp.dot(first_normed_rows.T, grad_q, preferred_element_type=jnp.float32), jnp.dot(first_normed_rows.T, grad_k, preferred_element_type=jnp.float32), jnp.dot(first_normed_rows.T, grad_v, preferred_element_type=jnp.float32)])
    first_normed_gradient = jnp.dot(grad_q, qkv_weight[0].T, preferred_element_type=jnp.float32)
    first_normed_gradient = first_normed_gradient + jnp.dot(grad_k, qkv_weight[1].T, preferred_element_type=jnp.float32)
    first_normed_gradient = first_normed_gradient + jnp.dot(grad_v, qkv_weight[2].T, preferred_element_type=jnp.float32)
    gradient_norm1_gain = lax.optimization_barrier(jnp.sum(first_normed_gradient * first_unit_rows, axis=0))
    first_scaled_rows = first_norm_gain * first_normed_gradient
    input_gradient = hidden_gradient + first_inverse_norm * (first_scaled_rows - first_unit_rows * lax.optimization_barrier(jnp.mean(first_scaled_rows * first_unit_rows, axis=-1, keepdims=True)))
    return (output, input_gradient, gradient_norm1_gain, grad_qkv_weight, grad_rel_bias, grad_out_weight, gradient_norm2_gain, grad_router_weight, grad_expert_up, grad_expert_down)
```

```python
import jax
import numpy as np
import jax.numpy as jnp
from jax import lax
from jax.experimental import pallas as pl
from jax.sharding import PartitionSpec as P
from jax.experimental.pallas import tpu as pltpu

HD = 64
MASKED = -1e30
F32 = jnp.float32
BF16 = jnp.bfloat16


def nn(a, b):
    return lax.dot_general(a, b, (((1,), (0,)), ((), ())), preferred_element_type=F32)


def nt(a, b):
    return lax.dot_general(a, b, (((1,), (1,)), ((), ())), preferred_element_type=F32)


def tile_kernel(rev_ref, fwd_ref, tile_ref, flip_ref):
    heads, rows = tile_ref.shape[1], tile_ref.shape[2]
    for h in range(heads):
        for src, dst in ((rev_ref, tile_ref), (fwd_ref, flip_ref)):
            base = jnp.broadcast_to(src[0, h], (8, 2 * rows))
            base = pltpu.roll(base, 0, 1, stride=1, stride_axis=0)
            for b in range(rows // 8):
                shift = (rows + 1 + 8 * b) % (2 * rows)
                dst[0, h, 8 * b : 8 * b + 8, :] = pltpu.roll(base, shift, 1)[:, :rows]


def make_tiles(rev, fwd):
    tiles, heads, _, width = rev.shape
    half = width // 2
    spec = pl.BlockSpec((1, heads, 1, width), lambda i: (i, 0, 0, 0))
    out = pl.BlockSpec((1, heads, half, half), lambda i: (i, 0, 0, 0))
    shape = jax.ShapeDtypeStruct((tiles, heads, half, half), F32)
    return pl.pallas_call(
        tile_kernel, grid=(tiles,), in_specs=[spec, spec], out_specs=[out, out],
        out_shape=[shape, shape], name="bias_tiles",
    )(rev, fwd)


def to_heads(feature_major, dst, heads):
    padded = jnp.concatenate(
        [feature_major.astype(F32), jnp.zeros((-feature_major.shape[0] % 128, feature_major.shape[1]), F32)], axis=0)
    natural = jnp.transpose(padded)
    for h in range(heads):
        dst[h] = natural[:, HD * h : HD * h + HD].astype(BF16)


def to_columns(row):
    return jnp.transpose(jnp.broadcast_to(row, (128, row.shape[1])))


def twice(column, width):
    return jnp.concatenate([column] * (width // 128), axis=1)


def forward_kernel(tab, q_ref, kv_ref, bias_ref, out_ref, lse_ref, q_nat, m_ref, acc_ref):
    heads, half = bias_ref.shape[1], bias_ref.shape[2]
    columns = heads * HD
    pair = pl.program_id(0)

    @pl.when(pair == 0)
    def _():
        to_heads(q_ref[...], q_nat, heads)
        m_ref[...] = jnp.full(m_ref.shape, MASKED, F32)
        acc_ref[...] = jnp.zeros(acc_ref.shape, F32)

    rows = pl.ds(pl.multiple_of(tab[0, pair] * half, half), half)
    ones = jnp.ones((128 - HD, half), BF16)
    for h in range(heads):
        s = nn(q_nat[h, rows, :], kv_ref[0, HD * h : HD * h + HD, :]) + bias_ref[0, h]
        m_old = m_ref[h, rows, :]
        m_new = jnp.maximum(m_old, jnp.max(s, axis=1, keepdims=True))
        p = jnp.exp(s - twice(m_new, half))
        v_ext = jnp.concatenate([kv_ref[0, columns + HD * h : columns + HD * h + HD, :], ones], axis=0)
        acc_ref[h, rows, :] = acc_ref[h, rows, :] * jnp.exp(m_old - m_new) + nt(p.astype(BF16), v_ext)
        m_ref[h, rows, :] = m_new

    @pl.when(pair == pl.num_programs(0) - 1)
    def _():
        for h in range(heads):
            turned = jnp.transpose(acc_ref[h])
            total = turned[HD : HD + 1, :]
            out_ref[HD * h : HD * h + HD, :] = (turned[:HD, :] / total).astype(BF16)
            lse_ref[h : h + 1, :] = jnp.transpose(m_ref[h])[:1, :] + jnp.log(total)


def attend(tab, q_t, kv, bias):
    pairs = tab.shape[1]
    _, heads, half, _ = bias.shape
    columns, rows = q_t.shape
    return pl.pallas_call(
        forward_kernel,
        grid_spec=pltpu.PrefetchScalarGridSpec(
            num_scalar_prefetch=1, grid=(pairs,),
            in_specs=[
                pl.BlockSpec((columns, rows), lambda p, t: (0, 0)),
                pl.BlockSpec((1, 2 * columns, half), lambda p, t: (t[1, p], 0, t[2, p])),
                pl.BlockSpec((1, heads, half, half), lambda p, t: (t[3, p], 0, 0, 0)),
            ],
            out_specs=[
                pl.BlockSpec((columns, rows), lambda p, t: (0, 0)),
                pl.BlockSpec((8, rows), lambda p, t: (0, 0)),
            ],
            scratch_shapes=[
                pltpu.VMEM((heads, rows, HD), BF16),
                pltpu.VMEM((heads, rows, 128), F32),
                pltpu.VMEM((heads, rows, 128), F32),
            ]),
        out_shape=[jax.ShapeDtypeStruct((columns, rows), BF16), jax.ShapeDtypeStruct((8, rows), F32)],
        name="attend",
    )(tab, q_t, kv, bias)


def query_kernel(tab, q_ref, do_ref, lse_ref, delta_ref, kv_ref, bias_ref, dq_ref, diag_ref,
                 q_nat, do_nat, lse_col, delta_col, acc_ref):
    heads, half = bias_ref.shape[1], bias_ref.shape[2]
    columns = heads * HD
    pair = pl.program_id(0)

    @pl.when(pair == 0)
    def _():
        to_heads(q_ref[...], q_nat, heads)
        to_heads(do_ref[...], do_nat, heads)
        for h in range(heads):
            lse_col[h] = to_columns(lse_ref[h : h + 1, :])
            delta_col[h] = to_columns(delta_ref[h : h + 1, :])
        acc_ref[...] = jnp.zeros(acc_ref.shape, F32)

    rows = pl.ds(pl.multiple_of(tab[0, pair] * half, half), half)
    for h in range(heads):
        k_t = kv_ref[0, HD * h : HD * h + HD, :]
        v_t = kv_ref[0, columns + HD * h : columns + HD * h + HD, :]
        s = nn(q_nat[h, rows, :], k_t) + bias_ref[0, h]
        p = jnp.exp(s - twice(lse_col[h, rows, :], half))
        ds = p * (nn(do_nat[h, rows, :], v_t) - twice(delta_col[h, rows, :], half))
        acc_ref[h, rows, :] += nt(ds.astype(BF16), k_t)
        total = jnp.zeros((8, 2 * half), F32)
        steps = 128 // 8
        for b in range(steps):
            piece = jnp.zeros((8, 2 * half), F32)
            for over in range(half // 128):
                at = 128 * over + 8 * b
                moved = ds[at : at + 8, :]
                left = 128 * over
                piece = piece + jnp.concatenate(
                    [moved[:, left:], jnp.zeros((8, half), F32), moved[:, :left]] if left else [moved, jnp.zeros((8, half), F32)], axis=1)
            total = total + (pltpu.roll(piece, 2 * half - 8 * b, 1) if b else piece)
        diag_ref[0, h] = total

    @pl.when(pair == pl.num_programs(0) - 1)
    def _():
        dq_ref[...] = jnp.concatenate([acc_ref[h] * HD ** (-0.5) for h in range(heads)], axis=1).astype(BF16)


def query_side(tab, q_t, do_t, lse, delta, kv, bias):
    pairs = tab.shape[1]
    _, heads, half, _ = bias.shape
    columns, rows = q_t.shape
    whole = lambda p, t: (0, 0)
    return pl.pallas_call(
        query_kernel,
        grid_spec=pltpu.PrefetchScalarGridSpec(
            num_scalar_prefetch=1, grid=(pairs,),
            in_specs=[
                pl.BlockSpec((columns, rows), whole),
                pl.BlockSpec((columns, rows), whole),
                pl.BlockSpec((8, rows), whole),
                pl.BlockSpec((8, rows), whole),
                pl.BlockSpec((1, 2 * columns, half), lambda p, t: (t[1, p], 0, t[2, p])),
                pl.BlockSpec((1, heads, half, half), lambda p, t: (t[3, p], 0, 0, 0)),
            ],
            out_specs=[
                pl.BlockSpec((rows, columns), whole),
                pl.BlockSpec((1, heads, 8, 2 * half), lambda p, t: (p, 0, 0, 0)),
            ],
            scratch_shapes=[
                pltpu.VMEM((heads, rows, HD), BF16),
                pltpu.VMEM((heads, rows, HD), BF16),
                pltpu.VMEM((heads, rows, 128), F32),
                pltpu.VMEM((heads, rows, 128), F32),
                pltpu.VMEM((heads, rows, HD), F32),
            ]),
        out_shape=[jax.ShapeDtypeStruct((rows, columns), BF16),
                   jax.ShapeDtypeStruct((pairs, heads, 8, 2 * half), F32)],
        name="query_side",
    )(tab, q_t, do_t, lse, delta, kv, bias)


def key_kernel(tab, kv_ref, q_ref, do_ref, lse_ref, delta_ref, bias_ref, dk_ref, dv_ref,
               k_nat, v_nat, dk_acc, dv_acc):
    heads, half = bias_ref.shape[1], bias_ref.shape[2]
    columns = heads * HD
    pair = pl.program_id(0)

    @pl.when(pair == 0)
    def _():
        to_heads(kv_ref[:columns, :], k_nat, heads)
        to_heads(kv_ref[columns:, :], v_nat, heads)
        dk_acc[...] = jnp.zeros(dk_acc.shape, F32)
        dv_acc[...] = jnp.zeros(dv_acc.shape, F32)

    rows = pl.ds(pl.multiple_of(tab[0, pair] * half, half), half)
    for h in range(heads):
        q_t = q_ref[0, HD * h : HD * h + HD, :]
        do_t = do_ref[0, HD * h : HD * h + HD, :]
        s = nn(k_nat[h, rows, :], q_t) + bias_ref[0, h]
        p = jnp.exp(s - lse_ref[0, h : h + 1, :])
        dv_acc[h, rows, :] += nt(p.astype(BF16), do_t)
        ds = p * (nn(v_nat[h, rows, :], do_t) - delta_ref[0, h : h + 1, :])
        dk_acc[h, rows, :] += nt(ds.astype(BF16), q_t)

    @pl.when(pair == pl.num_programs(0) - 1)
    def _():
        dk_ref[...] = jnp.concatenate([dk_acc[h] for h in range(heads)], axis=1).astype(BF16)
        dv_ref[...] = jnp.concatenate([dv_acc[h] for h in range(heads)], axis=1).astype(BF16)


def key_side(tab, kv_own, q_all, do_all, lse_all, delta_all, bias):
    pairs = tab.shape[1]
    _, heads, half, _ = bias.shape
    columns, rows = kv_own.shape[0] // 2, kv_own.shape[1]
    whole = lambda p, t: (0, 0)
    at = lambda p, t: (t[1, p], 0, t[2, p])
    return pl.pallas_call(
        key_kernel,
        grid_spec=pltpu.PrefetchScalarGridSpec(
            num_scalar_prefetch=1, grid=(pairs,),
            in_specs=[
                pl.BlockSpec((2 * columns, rows), whole),
                pl.BlockSpec((1, columns, half), at),
                pl.BlockSpec((1, columns, half), at),
                pl.BlockSpec((1, 8, half), at),
                pl.BlockSpec((1, 8, half), at),
                pl.BlockSpec((1, heads, half, half), lambda p, t: (t[3, p], 0, 0, 0)),
            ],
            out_specs=[pl.BlockSpec((rows, columns), whole)] * 2,
            scratch_shapes=[
                pltpu.VMEM((heads, rows, HD), BF16),
                pltpu.VMEM((heads, rows, HD), BF16),
                pltpu.VMEM((heads, rows, HD), F32),
                pltpu.VMEM((heads, rows, HD), F32),
            ]),
        out_shape=[jax.ShapeDtypeStruct((rows, columns), BF16)] * 2,
        name="key_side",
    )(tab, kv_own, q_all, do_all, lse_all, delta_all, bias)


NORM_EPS = 1e-06
ALL = ("ctx", "sx", "sc")
SHARD = ("sx", "sc")
SWAP = ((0, 1), (1, 0))


def bucket_numbers(distance):
    square = np.maximum(distance, 0).astype(np.int64) ** 2
    counted = sum((square >= 256 << j).astype(np.int32) for j in range(1, 16))
    return np.where(distance < 16, np.maximum(distance, 0), 16 + counted).astype(np.int32)


def tile_count(groups, half):
    count = 1
    while count < 2 * groups and ((count - 1) * half - half + 1) ** 2 * (count > 1) < 256 << 15:
        count += 1
    return count


def ring_of(size):
    return list(range(0, size, 2)) + list(range(size - 1, 0, -2))


def ring_gather(arrays, ring):
    size = len(ring)
    forth = [(ring[i], ring[(i + 1) % size]) for i in range(size)]
    back = [(b, a) for a, b in forth]
    slots = [tuple(arrays)]
    left, right = tuple(arrays), tuple(arrays)
    for hop in range(1, size // 2 + 1):
        left = tuple(lax.ppermute(a, "ctx", forth) for a in left)
        slots.append(left)
        if hop < size // 2:
            right = tuple(lax.ppermute(a, "ctx", back) for a in right)
            slots.append(right)
    return slots


def ring_groups(own, ring):
    size = len(ring)
    order = jnp.asarray(ring, jnp.int32)
    place = jnp.argmax(order == own).astype(jnp.int32)
    offsets = [0]
    for hop in range(1, size // 2 + 1):
        offsets.append(-hop)
        if hop < size // 2:
            offsets.append(hop)
    wanted = (place + jnp.asarray(offsets, jnp.int32)) % size
    return jnp.sum(jnp.where(wanted[:, None] == jnp.arange(size)[None, :], order[None, :], 0), axis=1)


def pair_tables(own, slot_groups, groups, tiles):
    last = 2 * groups - 1
    count = slot_groups.shape[0]
    other = slot_groups[1:]
    slot = jnp.arange(1, count, dtype=jnp.int32)
    zero, one = jnp.zeros_like(slot), jnp.ones_like(slot)
    before = (other < own).astype(jnp.int32)
    own_pairs = [[0, 0, 0, 0], [1, 0, 1, 0], [1, 0, 0, last - 2 * own]]
    head = jnp.stack([jnp.stack([jnp.asarray(v, jnp.int32) for v in row]) for row in own_pairs], axis=1)
    first = jnp.stack([one, slot, zero, last - own - other])
    second = jnp.stack([1 - before, slot, 1 - before, jnp.abs(own - other)])
    rest = jnp.stack([first, second], axis=2).reshape(4, -1)
    query = jnp.concatenate([head, rest], axis=1)
    key_head = jnp.stack([head[2], head[1], head[0], head[3]])
    key_first = jnp.stack([zero, slot, one, last - own - other])
    key_second = jnp.stack([before, slot, before, jnp.abs(own - other)])
    key_rest = jnp.stack([key_first, key_second], axis=2).reshape(4, -1)
    key = jnp.concatenate([key_head, key_rest], axis=1)
    cap = lambda t: jnp.concatenate([t[:3], jnp.minimum(t[3:], tiles - 1)], axis=0)
    return cap(query), cap(key)


def gather_shard(value, sx, sc):
    across = lax.ppermute(value, "sx", SWAP)
    low, high = jnp.where(sx == 0, value, across), jnp.where(sx == 0, across, value)
    pair = jnp.stack([low, high])
    other = lax.ppermute(pair, "sc", SWAP)
    even, odd = jnp.where(sc == 0, pair, other), jnp.where(sc == 0, other, pair)
    return jnp.stack([even, odd], axis=1).reshape((4,) + value.shape)


def scatter_shard(parts, sx, sc):
    split = parts.reshape((2, 2, parts.shape[0] // 4) + parts.shape[1:])
    kept = lax.dynamic_index_in_dim(split, sc, 1, False)
    sent = lax.dynamic_index_in_dim(split, 1 - sc, 1, False).astype(BF16)
    both = kept + lax.ppermute(sent, "sc", SWAP).astype(F32)
    mine = lax.dynamic_index_in_dim(both, sx, 0, False)
    theirs = lax.dynamic_index_in_dim(both, 1 - sx, 0, False).astype(BF16)
    return mine + lax.ppermute(theirs, "sx", SWAP).astype(F32)


def dot(a, b, ca, cb):
    return lax.dot_general(a, b, (((ca,), (cb,)), ((), ())), preferred_element_type=F32)


def gelu(u):
    return jax.nn.gelu(u, approximate=True)


def exchange(value):
    return lax.all_to_all(value, ALL, split_axis=0, concat_axis=0, tiled=True)


def sum_over_ctx(value, groups):
    pieces = value.astype(BF16).reshape((groups, value.shape[0] // groups) + value.shape[1:])
    mine = jnp.sum(lax.all_to_all(pieces, "ctx", 0, 0, tiled=True).astype(F32), axis=0).astype(BF16)
    return mine


def body(ring, layer_input, norm1_gain, qkv_weight, rel_bias, out_weight, norm2_gain, router_weight,
         expert_up, expert_down, routes, cotangent):
    groups = len(ring)
    own, sx, sc = lax.axis_index("ctx"), lax.axis_index("sx"), lax.axis_index("sc")
    tok, width = layer_input.shape
    heads = rel_bias.shape[1]
    columns = heads * HD
    experts, local = router_weight.shape[1], expert_up.shape[0]
    capacity = 4 * tok // experts
    rows = 4 * tok
    half = rows // 2

    gains = jnp.concatenate([norm1_gain, norm2_gain, jnp.zeros((width - 2 * norm1_gain.shape[0],), BF16)])
    packed = jnp.concatenate([layer_input, jnp.broadcast_to(gains, (16, width))], axis=0)
    gathered = gather_shard(packed, sx, sc)
    quarter = norm1_gain.shape[0]
    gain1 = gathered[:, tok, :quarter].reshape(-1).astype(F32)
    gain2 = gathered[:, tok, quarter : 2 * quarter].reshape(-1).astype(F32)
    group_x = gathered[:, :tok].reshape(rows, width).astype(F32)
    router = gather_shard(router_weight, sx, sc).reshape(width, experts)

    tiles = tile_count(groups, half)
    place = np.arange(2 * half)
    spread = np.arange(tiles)[:, None] * half + place[None, :] - half + 1
    numbers = bucket_numbers(spread)
    flipped_place = (2 * half - 2 - place) % (2 * half)
    names = jnp.arange(rel_bias.shape[0], dtype=jnp.int32)

    def line(ids, distances):
        hot = (jnp.asarray(ids)[..., None] == names).astype(F32)
        values = jnp.einsum("tck,kh->thc", hot, rel_bias, precision=lax.Precision.HIGHEST)
        return jnp.where(jnp.asarray(distances < 0)[:, None, :], MASKED, values)[:, :, None, :]

    tile, flip = make_tiles(line(numbers[:, flipped_place], spread[:, flipped_place]), line(numbers, spread))
    slot_groups = ring_groups(own, ring)
    query_table, key_table = pair_tables(own, slot_groups, groups, tiles)

    flat_routes = routes.reshape(-1)
    hits = (flat_routes[:, None] == jnp.arange(experts, dtype=jnp.int32)).astype(BF16)
    earlier = jnp.asarray(np.tril(np.ones((2 * tok, 2 * tok), np.float32), -1), BF16)
    ranks = jnp.sum(dot(earlier, hits, 1, 0) * hits.astype(F32), axis=1).astype(jnp.int32)
    slot = (flat_routes * capacity + ranks).reshape(tok, 2)
    ids = jnp.arange(experts * capacity, dtype=jnp.int32)
    pick = [(slot[:, k][:, None] == ids[None, :]).astype(BF16) for k in range(2)]
    either = pick[0] + pick[1]
    devices = 2 * experts
    share = experts * capacity // devices

    def dispatch(token_rows):
        return exchange(dot(either, token_rows, 0, 0).astype(BF16).reshape(devices, share, width)).reshape(-1, width)

    def both_halves(value):
        other = lax.ppermute(value, "sc", SWAP)
        return jnp.concatenate([value, other], axis=0)

    cot_rows = both_halves(dispatch(cotangent))

    def swap_weights(weight):
        kept = lax.dynamic_index_in_dim(weight, sx, 0, False)
        return kept, lax.ppermute(lax.dynamic_index_in_dim(weight, 1 - sx, 0, False), "sx", SWAP)

    up = jnp.concatenate(swap_weights(expert_up), axis=1)
    down = jnp.concatenate(swap_weights(expert_down), axis=0)

    normed_group = (group_x * lax.rsqrt(jnp.mean(group_x * group_x, axis=-1, keepdims=True) + NORM_EPS) * gain1).astype(BF16)
    joined = jnp.concatenate([qkv_weight[0], qkv_weight[1], qkv_weight[2]], axis=1)
    projected = dot(joined, normed_group, 0, 1).astype(BF16)
    q_t = projected[:columns] * BF16(HD ** (-0.5))
    kv_own = projected[columns:]
    kv = jnp.stack([s[0] for s in ring_gather((kv_own,), ring)])
    attn_t, lse = attend(query_table, q_t, kv, tile)
    q_slots = ring_gather((q_t, lse), ring)
    q_all, lse_all = jnp.stack([s[0] for s in q_slots]), jnp.stack([s[1] for s in q_slots])
    x_own = layer_input.astype(F32)
    hidden = x_own + scatter_shard(dot(attn_t, out_weight, 0, 0), sx, sc)

    inverse2 = lax.rsqrt(jnp.mean(hidden * hidden, axis=-1, keepdims=True) + NORM_EPS)
    unit2 = hidden * inverse2
    normed2 = (unit2 * gain2).astype(BF16)
    probs = jax.nn.softmax(dot(normed2, router, 1, 0), axis=-1)
    chosen = [(routes[:, k : k + 1] == jnp.arange(experts, dtype=jnp.int32)[None, :]) for k in range(2)]
    gates = [jnp.sum(jnp.where(chosen[k], probs, 0.0), axis=1, keepdims=True) for k in range(2)]
    x_rows = both_halves(dispatch(normed2))
    inner = dot(x_rows, up, 1, 0)
    act, act_vjp = jax.vjp(gelu, inner)
    act = act.astype(BF16)
    mine = jnp.arange(experts, dtype=jnp.int32)[None, :] == 2 * own + sx
    row_gate = jnp.sum(jnp.where(mine, jax.nn.softmax(dot(x_rows, router, 1, 0), axis=-1), 0.0), axis=1, keepdims=True)
    grad_rows = (row_gate * cot_rows.astype(F32)).astype(BF16)
    grad_inner = act_vjp(dot(grad_rows, down, 1, 1))[0].astype(BF16)

    def send_back(parts):
        count = parts.shape[0] // 2
        other = lax.ppermute(parts[count:].astype(BF16), "sc", SWAP)
        total = (parts[:count] + other.astype(F32)).astype(BF16)
        return exchange(total.reshape(devices, share, width)).reshape(-1, width)

    returned = send_back(dot(act, down, 1, 0))
    grad_returned = send_back(dot(grad_inner, up, 1, 1))
    grad_down = dot(act, grad_rows, 0, 0)
    grad_up = dot(x_rows, grad_inner, 0, 0)

    def owners(value, axis):
        cut = value.shape[axis] // 2
        kept = lax.slice_in_dim(value, 0, cut, axis=axis)
        got = lax.ppermute(lax.slice_in_dim(value, cut, 2 * cut, axis=axis).astype(BF16), "sx", SWAP).astype(F32)
        return jnp.stack([jnp.where(sx == 0, kept, got), jnp.where(sx == 0, got, kept)])

    grad_up_own, grad_down_own = owners(grad_up, 1), owners(grad_down, 0)

    upstream = cotangent.astype(F32)
    rows_k = [dot(pick[k], returned, 1, 0) for k in range(2)]
    output = hidden + gates[0] * rows_k[0] + gates[1] * rows_k[1]
    grad_gate = [jnp.sum(upstream * rows_k[k], axis=1, keepdims=True) for k in range(2)]
    from_experts = dot(either, grad_returned, 1, 0)
    grad_probs = jnp.where(chosen[0], grad_gate[0], 0.0) + jnp.where(chosen[1], grad_gate[1], 0.0)
    grad_logits = (probs * (grad_probs - jnp.sum(probs * grad_probs, axis=-1, keepdims=True))).astype(BF16)
    grad_router = dot(normed2, grad_logits, 0, 0)
    grad_normed2 = dot(grad_logits, router, 1, 1) + from_experts
    grad_gain2 = jnp.sum(grad_normed2 * unit2, axis=0)
    scaled2 = gain2 * grad_normed2
    grad_hidden = upstream + inverse2 * (scaled2 - unit2 * jnp.mean(scaled2 * unit2, axis=-1, keepdims=True))

    grad_group = gather_shard(grad_hidden.astype(BF16), sx, sc).reshape(rows, width)
    do_t = dot(out_weight, grad_group, 1, 1).astype(BF16)
    grad_out = dot(attn_t, grad_group, 1, 0)
    delta = jnp.sum((do_t.astype(F32) * attn_t.astype(F32)).reshape(heads, HD, rows), axis=1)
    delta = jnp.concatenate([delta, jnp.zeros((8 - heads, rows), F32)], axis=0)
    do_slots = ring_gather((do_t, delta), ring)
    do_all, delta_all = jnp.stack([s[0] for s in do_slots]), jnp.stack([s[1] for s in do_slots])
    grad_q, diagonals = query_side(query_table, q_t, do_t, lse, delta, kv, tile)
    grad_k, grad_v = key_side(key_table, kv_own, q_all, do_all, lse_all, delta_all, flip)

    offset = np.where(place < half, place, place - 2 * half)
    spans = np.arange(tiles)[:, None, None] * half + np.arange(8)[None, :, None] - offset[None, None, :]
    span_ids = jnp.take(jnp.asarray(bucket_numbers(spans)), query_table[3], axis=0)
    hot = (span_ids[..., None] == names).astype(F32)
    grad_table = jnp.einsum("phrc,prck->kh", diagonals, hot, precision=lax.Precision.HIGHEST)

    grad_joined = jnp.concatenate([grad_q, grad_k, grad_v], axis=1)
    grad_qkv = dot(normed_group, grad_joined, 0, 0)
    grad_normed1 = scatter_shard(dot(grad_joined, joined, 1, 1), sx, sc)
    inverse1 = lax.rsqrt(jnp.mean(x_own * x_own, axis=-1, keepdims=True) + NORM_EPS)
    unit1 = x_own * inverse1
    grad_gain1 = jnp.sum(grad_normed1 * unit1, axis=0)
    scaled1 = gain1 * grad_normed1
    input_gradient = grad_hidden + inverse1 * (scaled1 - unit1 * jnp.mean(scaled1 * unit1, axis=-1, keepdims=True))

    def ctx_order(slots):
        out = jnp.zeros((groups,) + slots[0].shape, slots[0].dtype)
        for i in range(groups):
            out = lax.dynamic_update_index_in_dim(out, slots[i], slot_groups[i], 0)
        return out

    sums = ring_gather((sum_over_ctx(grad_qkv, groups), sum_over_ctx(grad_out, groups)), ring)
    qkv_sum = ctx_order([s[0] for s in sums]).reshape(width, 3, columns).transpose(1, 0, 2).astype(F32)
    out_sum = ctx_order([s[1] for s in sums]).reshape(columns, width).astype(F32)

    small = jnp.concatenate([grad_router.T, grad_gain1[None], grad_gain2[None]], axis=0)
    small = small.reshape(experts + 2, 4, quarter).transpose(1, 0, 2)
    small = scatter_shard(small.reshape(4 * (experts + 2), quarter), sx, sc).astype(BF16)
    tail = ring_gather((small, grad_table.astype(BF16)), ring)
    small_sum = sum(s[0].astype(F32) for s in tail)
    table_sum = sum(s[1].astype(F32) for s in tail)
    return (output, input_gradient, small_sum[experts], qkv_sum, table_sum, out_sum, small_sum[experts + 1],
            small_sum[:experts].T, grad_up_own, grad_down_own)


def solution(mesh):
    ctx, shard = mesh.shape["ctx"], mesh.shape["shard"]
    inner = jax.sharding.Mesh(mesh.devices.reshape(ctx, shard // 2, 2), ALL)
    ring = ring_of(ctx)
    tokens = P(ALL, None)
    in_specs = (tokens, P(SHARD), P(None, None, SHARD), P(None, SHARD), P(SHARD, None), P(SHARD), P(SHARD, None),
                P("ctx", None, SHARD), P("ctx", SHARD, None), tokens, tokens)
    out_specs = (tokens, tokens, P(SHARD), P(None, None, SHARD), P(None, SHARD), P(SHARD, None), P(SHARD),
                 P(SHARD, None), P("ctx", None, SHARD), P("ctx", SHARD, None))
    return jax.shard_map(lambda *args: body(ring, *args), mesh=inner, in_specs=in_specs, out_specs=out_specs, check_vma=False)
```

```python
import jax
import numpy as np
import jax.numpy as jnp
from jax import lax
from jax.experimental import pallas as pl
from jax.sharding import PartitionSpec as P
from jax.experimental.pallas import tpu as pltpu

HD = 64
STATS = 16
MASKED = -1e30
F32 = jnp.float32
BF16 = jnp.bfloat16


def nn(a, b):
    return lax.dot_general(a, b, (((1,), (0,)), ((), ())), preferred_element_type=F32)


def nt(a, b):
    return lax.dot_general(a, b, (((1,), (1,)), ((), ())), preferred_element_type=F32)


def bias_of(line_ref, tile, head):
    width = line_ref.shape[2]
    half = width // 2
    base = jnp.broadcast_to(line_ref[tile, head : head + 1, :], (8, width))
    base = pltpu.roll(base, 0, 1, stride=1, stride_axis=0)
    moved = [pltpu.roll(base, (half + 1 + 8 * b) % width, 1) for b in range(128 // 8)]
    pieces = []
    for over in range(half // 128):
        cut = 128 * over
        for m in moved:
            pieces.append(jnp.concatenate([m[:, width - cut :], m[:, : half - cut]], axis=1) if over else m[:, :half])
    return jnp.concatenate(pieces, axis=0)


def to_heads(feature_major, dst, heads, extra=None):
    count, rows = feature_major.shape
    padded = jnp.concatenate([feature_major.astype(F32), jnp.zeros((-count % 128, rows), F32)], axis=0)
    natural = jnp.transpose(padded).astype(BF16)
    columns = heads * HD
    for h in range(heads):
        dst[h, :, :HD] = natural[:, HD * h : HD * h + HD]
        if extra is not None:
            dst[h, :, HD:] = natural[:, columns : columns + STATS] if extra == "stats" else picks(h, heads, (rows, STATS), 1)


def picks(head, heads, shape, axis):
    at = lax.broadcasted_iota(jnp.int32, shape, axis)
    return jnp.where((at % heads == head) & (at < 3 * heads), 1.0, 0.0).astype(BF16)


def pack_rows(values):
    high = lax.reduce_precision(values, 8, 7)
    rest = values - high
    mid = lax.reduce_precision(rest, 8, 7)
    low = rest - mid
    blank = jnp.zeros((STATS - 3 * values.shape[0], values.shape[1]), BF16)
    return jnp.concatenate([high.astype(BF16), mid.astype(BF16), low.astype(BF16), blank], axis=0)


HELD = pl.BlockSpec(memory_space=pltpu.VMEM)
TABLE = pl.BlockSpec(memory_space=pltpu.SMEM)
PARAMS = pltpu.CompilerParams(vmem_limit_bytes=24 << 20)


def entry_at(entries, side, kind, entry, step):
    return ((side * 3 + kind) * entries + entry) * 2 + step


def each_entry(count, alone, do):
    for step in range(2):
        for e in range(count):
            if e != alone or step == 0:
                do(e, step)


def in_turn(count, alone, heads, begin, finish):
    items = [(step, e, h) for step in range(2) for e in range(count) if e != alone or step == 0 for h in range(heads)]
    following = begin(*items[0])
    for number, item in enumerate(items):
        current = following
        if number + 1 < len(items):
            following = begin(*items[number + 1])
        finish(*item, *current)


def columns_at(ref, begin, count, at, half):
    return ref[begin : begin + count, pl.ds(pl.multiple_of(at * half, half), half)]


def forward_kernel(at, count, alone, first, last, tab, q_ref, *refs):
    kv_refs, line_ref, refs = refs[:count], refs[count], refs[count + 1 :]
    if not first:
        before_ref, refs = refs[0], refs[1:]
    if last:
        out_ref, lse_ref, k_nat, state = refs
    else:
        state, k_nat = refs
    heads, half = line_ref.shape[1], line_ref.shape[2] // 2
    columns = heads * HD

    for e in range(count):
        if e != alone:
            to_heads(kv_refs[e][:columns, :], k_nat.at[e], heads)
    if first:
        state[...] = jnp.zeros(state.shape, F32)
        for h in range(heads):
            state[h, HD + STATS :, :] = jnp.full((8, state.shape[2]), MASKED, F32)
    else:
        state[...] = before_ref[...]

    ones = jnp.ones((STATS, half), BF16)

    def spots(step, e):
        lanes = pl.ds(pl.multiple_of(tab[at(0, e, step)] * half, half), half)
        return lanes, tab[at(1, e, step)], tab[at(2, e, step)]

    def begin(step, e, h):
        lanes, side, _ = spots(step, e)
        rows = pl.ds(pl.multiple_of(side * half, half), half)
        return (nn(k_nat[0 if e == alone else e, h, rows, :], q_ref[HD * h : HD * h + HD, lanes]),)

    def finish(step, e, h, s):
        lanes, side, tile = spots(step, e)
        s = s + bias_of(line_ref, tile, h)
        m_old = state[h, HD + STATS : HD + STATS + 1, lanes]
        m_new = jnp.maximum(m_old, jnp.max(s, axis=0, keepdims=True))
        p = jnp.exp(s - m_new)
        v_ext = jnp.concatenate([columns_at(kv_refs[e], columns + HD * h, HD, side, half), ones], axis=0)
        kept = state[h, : HD + STATS, lanes] * jnp.exp(m_old - m_new)
        state[h, : HD + STATS, lanes] = kept + nn(v_ext, p.astype(BF16))
        state[h, HD + STATS :, lanes] = jnp.broadcast_to(m_new, (8, half))

    in_turn(count, alone, heads, begin, finish)

    if last:
        for h in range(heads):
            total = state[h, HD : HD + 1, :]
            out_ref[HD * h : HD * h + HD, :] = (state[h, :HD, :] / total).astype(BF16)
            lse_ref[h : h + 1, :] = state[h, HD + STATS : HD + STATS + 1, :] + jnp.log(total)


def call(kernel, out_shape, scratch, *operands):
    many = isinstance(out_shape, list)
    return pl.pallas_call(
        kernel, out_shape=out_shape, out_specs=[HELD] * len(out_shape) if many else HELD,
        in_specs=[TABLE] + [HELD] * (len(operands) - 1), scratch_shapes=scratch, compiler_params=PARAMS,
    )(*operands)


def attend(tab, entries, begin, q_t, kvs, lines, state, last, alone=-1):
    at = lambda kind, e, p: entry_at(entries, 0, kind, begin + e, p)
    heads = lines.shape[1]
    columns, rows = q_t.shape
    kind = (heads, HD + STATS + 8, rows)
    first = state is None
    scratch = [pltpu.VMEM((len(kvs), heads, rows, HD), BF16)] + ([pltpu.VMEM(kind, F32)] if last else [])
    finished = [jax.ShapeDtypeStruct((columns, rows), BF16), jax.ShapeDtypeStruct((8, rows), F32)]
    return call(
        lambda *refs: forward_kernel(at, len(kvs), alone, first, last, *refs),
        finished if last else jax.ShapeDtypeStruct(kind, F32), scratch,
        tab, q_t, *kvs, lines, *(() if first else (state,)))


def query_kernel(at, count, alone, first, last, tab, q_ref, do_ref, *refs):
    kv_refs, line_ref, refs = refs[:count], refs[count], refs[count + 1 :]
    if not first:
        before_ref, refs = refs[0], refs[1:]
    out_ref, diag_ref, q_nat, do_nat = refs[:4]
    acc = refs[4] if last else out_ref
    heads, half = line_ref.shape[1], line_ref.shape[2] // 2
    columns = heads * HD

    to_heads(q_ref[...], q_nat, heads, "stats")
    to_heads(do_ref[...], do_nat, heads, "stats")
    if first:
        acc[...] = jnp.zeros(acc.shape, F32)
    else:
        acc[...] = before_ref[...]

    line = lax.broadcasted_iota(jnp.int32, (8, 2 * half), 0)
    blank = jnp.zeros((8, half), F32)
    chosen = [picks(h, heads, (STATS, half), 0) for h in range(heads)]

    if 0 <= alone:
        diag_ref[1, alone] = jnp.zeros(diag_ref.shape[2:], F32)

    def spots(step, e, h):
        side = tab[at(1, e, step)]
        k_t = columns_at(kv_refs[e], HD * h, HD, side, half)
        v_t = columns_at(kv_refs[e], columns + HD * h, HD, side, half)
        return pl.ds(pl.multiple_of(tab[at(0, e, step)] * half, half), half), k_t, v_t

    def begin(step, e, h):
        rows, k_t, v_t = spots(step, e, h)
        return (nn(q_nat[h, rows, :], jnp.concatenate([k_t, chosen[h]], axis=0)),
                nn(do_nat[h, rows, :], jnp.concatenate([v_t, chosen[h]], axis=0)))

    def finish(step, e, h, s, dp):
        rows, k_t, _ = spots(step, e, h)
        ds = jnp.exp(s + bias_of(line_ref, tab[at(2, e, step)], h)) * dp
        acc[h, rows, :] += nt(ds.astype(BF16), k_t)
        total = jnp.zeros((8, 2 * half), F32)
        for b in range(128 // 8):
            piece = jnp.concatenate([ds[8 * b : 8 * b + 8, :], blank], axis=1)
            for over in range(1, half // 128):
                cut = 128 * over
                moved = ds[cut + 8 * b : cut + 8 * b + 8, :]
                piece = piece + jnp.concatenate([moved[:, cut:], blank, moved[:, :cut]], axis=1)
            total = total + (pltpu.roll(piece, 2 * half - 8 * b, 1) if b else piece)
        for bit in (1, 2, 4):
            total = jnp.where((line & bit) != 0, pltpu.roll(total, 2 * half - bit, 1), total)
        diag_ref[step, e, h : h + 1, :] = jnp.sum(total, axis=0, keepdims=True)

    in_turn(count, alone, heads, begin, finish)

    if last:
        out_ref[...] = jnp.concatenate([acc[h] * HD ** (-0.5) for h in range(heads)], axis=1).astype(BF16)


def query_side(tab, entries, begin, q_ext, do_ext, kvs, lines, state, last, alone=-1):
    at = lambda kind, e, p: entry_at(entries, 0, kind, begin + e, p)
    heads, width = lines.shape[1], lines.shape[2]
    extended, rows = q_ext.shape
    kind = (heads, rows, HD)
    first = state is None
    scratch = [pltpu.VMEM((heads, rows, HD + STATS), BF16)] * 2
    out_kind = ((rows, extended - STATS), BF16) if last else (kind, F32)
    return call(
        lambda *refs: query_kernel(at, len(kvs), alone, first, last, *refs),
        [jax.ShapeDtypeStruct(*out_kind), jax.ShapeDtypeStruct((2, len(kvs), heads, width), F32)],
        scratch + ([pltpu.VMEM(kind, F32)] if last else []),
        tab, q_ext, do_ext, *kvs, lines, *(() if first else (state,)))


def key_kernel(at, count, alone, first, last, tab, kv_ref, *refs):
    q_refs, do_refs, line_ref, refs = refs[:count], refs[count : 2 * count], refs[2 * count], refs[2 * count + 1 :]
    if not first:
        before_ref, refs = refs[0], refs[1:]
    if last:
        dk_ref, dv_ref, k_nat, v_nat, state = refs
    else:
        state, k_nat, v_nat = refs
    heads, half = line_ref.shape[1], line_ref.shape[2] // 2
    columns = heads * HD

    to_heads(kv_ref[:columns, :], k_nat, heads, "picks")
    to_heads(kv_ref[columns:, :], v_nat, heads, "picks")
    if first:
        state[...] = jnp.zeros(state.shape, F32)
    else:
        state[...] = before_ref[...]

    def do(e, step):
        rows = pl.ds(pl.multiple_of(tab[at(0, e, step)] * half, half), half)
        q_ref, do_ref, side, tile = q_refs[e], do_refs[e], tab[at(1, e, step)], tab[at(2, e, step)]
        lse, delta = columns_at(q_ref, columns, STATS, side, half), columns_at(do_ref, columns, STATS, side, half)
        for h in range(heads):
            q_t = columns_at(q_ref, HD * h, HD, side, half)
            do_t = columns_at(do_ref, HD * h, HD, side, half)
            p = jnp.exp(nn(k_nat[h, rows, :], jnp.concatenate([q_t, lse], axis=0)) + bias_of(line_ref, tile, h))
            state[1, h, rows, :] += nt(p.astype(BF16), do_t)
            ds = p * nn(v_nat[h, rows, :], jnp.concatenate([do_t, delta], axis=0))
            state[0, h, rows, :] += nt(ds.astype(BF16), q_t)

    each_entry(count, alone, do)

    if last:
        dk_ref[...] = jnp.concatenate([state[0, h] for h in range(heads)], axis=1).astype(BF16)
        dv_ref[...] = jnp.concatenate([state[1, h] for h in range(heads)], axis=1).astype(BF16)


def key_side(tab, entries, begin, kv_own, qs, dos, lines, state, last, alone=-1):
    at = lambda kind, e, p: entry_at(entries, 1, kind, begin + e, p)
    heads = lines.shape[1]
    columns, rows = kv_own.shape[0] // 2, kv_own.shape[1]
    kind = (2, heads, rows, HD)
    first = state is None
    finished = [jax.ShapeDtypeStruct((rows, columns), BF16)] * 2
    return call(
        lambda *refs: key_kernel(at, len(qs), alone, first, last, *refs),
        finished if last else jax.ShapeDtypeStruct(kind, F32),
        [pltpu.VMEM((heads, rows, HD + STATS), BF16)] * 2 + ([pltpu.VMEM(kind, F32)] if last else []),
        tab, kv_own, *qs, *dos, lines, *(() if first else (state,)))


CURVE = 0.7978845608028654


def expert_kernel(mine_ref, own_ref, other_ref, up_a, up_b, grad_a, grad_b, router_ref,
                  act_a, act_b, inner_a, inner_b, kept_ref, sent_ref, stats_ref, *, block, experts):
    count, width = own_ref.shape
    at_expert = lax.broadcasted_iota(jnp.int32, (block, router_ref.shape[1]), 1)
    at_lane = lax.broadcasted_iota(jnp.int32, (block, 128), 1)
    for tile in range(2 * count // block):
        source = own_ref if tile * block < count else other_ref
        place = pl.ds(tile * block % count, block)
        rows = pl.ds(tile * block, block)
        x = source[place, :]
        logits = jnp.where(at_expert < experts, nn(x, router_ref[...]), MASKED)
        powers = jnp.exp(logits - jnp.max(logits, axis=1, keepdims=True))
        share = jnp.sum(jnp.where(at_expert == mine_ref[0], powers, 0.0), axis=1, keepdims=True)
        gate = share / jnp.sum(powers, axis=1, keepdims=True)
        back = jnp.zeros((block, width), F32)
        paid = jnp.zeros((block, 128), F32)
        steps = [(up, grads, act_ref, inner_ref, slice(cut, cut + 256))
                 for up, grads, act_ref, inner_ref in ((up_a, grad_a, act_a, inner_a), (up_b, grad_b, act_b, inner_b))
                 for cut in range(0, up.shape[1], 256)]
        following = nn(x, steps[0][0][:, steps[0][4]])
        for number, (up, grads, act_ref, inner_ref, piece) in enumerate(steps):
            u = following
            if number + 1 < len(steps):
                following = nn(x, steps[number + 1][0][:, steps[number + 1][4]])
            square = u * u
            t = jnp.tanh(u * (CURVE + (CURVE * 0.044715) * square))
            high = 0.5 + 0.5 * t
            act = (u * high).astype(BF16)
            act_ref[rows, piece] = act
            slope = high + u * (high * (1.0 - t)) * (CURVE + (CURVE * 0.134145) * square)
            g = grads[rows, piece].astype(F32)
            inner = (gate * (g * slope)).astype(BF16)
            inner_ref[rows, piece] = inner
            back = back + nt(inner, up[:, piece])
            product = act.astype(F32) * g
            paid = paid + product[:, :128] + product[:, 128:]
        paid = jnp.sum(paid, axis=1, keepdims=True)
        if tile * block < count:
            kept_ref[place, :width] = back
            kept_ref[place, width:] = jnp.where(at_lane == 0, paid, 0.0)
        else:
            high = paid.astype(BF16).astype(F32)
            sent_ref[place, :width] = back.astype(BF16)
            sent_ref[place, width:] = jnp.where(at_lane == 0, high, jnp.where(at_lane == 1, paid - high, 0.0)).astype(BF16)
        stats_ref[rows, :] = jnp.broadcast_to(gate, (block, 128))


def expert_front(mine, own, other, ups, grads, router):
    count, width = own.shape
    hidden = ups[0].shape[1]
    rows = 2 * count
    experts = router.shape[1]
    router = jnp.concatenate([router, jnp.zeros((width, -experts % 128), BF16)], axis=1)
    wide = [jax.ShapeDtypeStruct((rows, hidden), BF16)] * 4
    return pl.pallas_call(
        lambda *refs: expert_kernel(*refs, block=256, experts=experts), name="expert_front",
        in_specs=[TABLE] + [HELD] * 7, out_specs=[HELD] * 7,
        out_shape=wide + [jax.ShapeDtypeStruct((count, width + 128), F32), jax.ShapeDtypeStruct((count, width + 128), BF16),
                          jax.ShapeDtypeStruct((rows, 128), F32)],
        compiler_params=pltpu.CompilerParams(vmem_limit_bytes=32 << 20),
    )(mine, own, other, *ups, *grads, router)


NORM_EPS = 1e-06
ALL = ("ctx", "sx", "sc")
SHARD = ("sx", "sc")
SWAP = ((0, 1), (1, 0))


def bucket_numbers(distance):
    square = np.maximum(distance, 0).astype(np.int64) ** 2
    counted = sum((square >= 256 << j).astype(np.int32) for j in range(1, 16))
    return np.where(distance < 16, np.maximum(distance, 0), 16 + counted).astype(np.int32)


def tile_count(groups, half):
    count = 2
    while count < 2 * groups and ((count - 1) * half - half + 1) ** 2 < 256 << 15:
        count += 1
    return count


def ring_of(size):
    return list(range(0, size, 2)) + list(range(size - 1, 0, -2))


def ring_steps(size):
    steps = []
    for hop in range(1, size // 2 + 1):
        steps.append(-hop)
        if hop < size // 2:
            steps.append(hop)
    return steps


def entry_tables(ring, tiles):
    size = len(ring)
    top = 2 * size - 1
    place = {g: i for i, g in enumerate(ring)}
    tables = []
    for own in range(size):
        query = [[(0, 0, 0), (1, 1, 0)], [(1, 0, top - 2 * own)] * 2]
        key = [[(0, 0, 0), (1, 1, 0)], [(0, 1, top - 2 * own)] * 2]
        for step in ring_steps(size):
            other = ring[(place[own] + step) % size]
            if other < own:
                query.append([(1, 0, top - own - other), (0, 0, own - other)])
                key.append([(0, 1, top - own - other), (1, 1, own - other)])
            else:
                query.append([(1, 0, top - own - other), (1, 1, other - own)])
                key.append([(0, 1, top - own - other), (0, 0, other - own)])
        tables.append([query, key])
    table = np.array(tables, np.int32).transpose(0, 1, 4, 2, 3)
    table[:, :, 2] = np.minimum(table[:, :, 2], tiles - 1)
    slots = [[own] + [ring[(place[own] + step) % size] for step in ring_steps(size)] for own in range(size)]
    return np.concatenate([table.reshape(size, -1), np.array(slots, np.int32)], axis=1)


def ring_gather(value, ring):
    size = len(ring)
    forth = [(ring[i], ring[(i + 1) % size]) for i in range(size)]
    back = [(b, a) for a, b in forth]
    slots, left, right = [value], value, value
    for hop in range(1, size // 2 + 1):
        left = lax.ppermute(left, "ctx", forth)
        slots.append(left)
        if hop < size // 2:
            right = lax.ppermute(right, "ctx", back)
            slots.append(right)
    return slots


def gather_shard(value, is_x, is_c):
    across = lax.ppermute(value, "sx", SWAP)
    pair = jnp.stack([jnp.where(is_x, across, value), jnp.where(is_x, value, across)])
    other = lax.ppermute(pair, "sc", SWAP)
    return jnp.stack([jnp.where(is_c, other, pair), jnp.where(is_c, pair, other)], axis=1).reshape((4,) + value.shape)


def scatter_shard(parts, is_x, is_c):
    split = parts.reshape((2, 2, parts.shape[0] // 4) + parts.shape[1:])
    kept, sent = jnp.where(is_c, split[:, 1], split[:, 0]), jnp.where(is_c, split[:, 0], split[:, 1])
    both = kept + lax.ppermute(sent.astype(BF16), "sc", SWAP).astype(F32)
    mine, theirs = jnp.where(is_x, both[1], both[0]), jnp.where(is_x, both[0], both[1])
    return mine + lax.ppermute(theirs.astype(BF16), "sx", SWAP).astype(F32)


def dot(a, b, ca, cb):
    return lax.dot_general(a, b, (((ca,), (cb,)), ((), ())), preferred_element_type=F32)


def to_all(value, axes=ALL):
    return lax.all_to_all(value, axes, split_axis=0, concat_axis=0, tiled=True)


def after(value, *others):
    return lax.optimization_barrier((value,) + others)[0]


def body(ring, table, layer_input, norm1_gain, qkv_weight, rel_bias, out_weight, norm2_gain, router_weight,
         expert_up, expert_down, routes, cotangent):
    groups = len(ring)
    own, sx, sc = lax.axis_index("ctx"), lax.axis_index("sx"), lax.axis_index("sc")
    is_x, is_c = sx == 1, sc == 1
    tok, width = layer_input.shape
    buckets, heads = rel_bias.shape
    columns = heads * HD
    experts = router_weight.shape[1]
    capacity = 4 * tok // experts
    rows = 4 * tok
    half = rows // 2
    quarter = norm1_gain.shape[0]
    devices = 2 * experts
    share = experts * capacity // devices

    gains = jnp.concatenate([norm1_gain, norm2_gain, jnp.zeros((width - 2 * quarter,), BF16)])
    packed = jnp.concatenate([layer_input, jnp.broadcast_to(gains, (16, width))], axis=0)
    gathered = gather_shard(packed, is_x, is_c)
    gain1 = gathered[:, tok, :quarter].reshape(-1).astype(F32)
    gain2 = gathered[:, tok, quarter : 2 * quarter].reshape(-1).astype(F32)
    group_x = gathered[:, :tok].reshape(rows, width).astype(F32)

    tiles = tile_count(groups, half)
    place = np.arange(2 * half)
    spread = np.arange(tiles)[:, None] * half + place[None, :] - half + 1
    numbers = bucket_numbers(spread)
    turned = (2 * half - 2 - place) % (2 * half)
    names = jnp.arange(buckets, dtype=jnp.int32)

    def line(ids, distances):
        hot = (jnp.asarray(ids)[..., None] == names).astype(F32)
        values = jnp.einsum("tck,kh->thc", hot, rel_bias, precision=lax.Precision.HIGHEST)
        return jnp.where(jnp.asarray(distances < 0)[:, None, :], MASKED, values)

    lines, turned_lines = line(numbers, spread), line(numbers[:, turned], spread[:, turned])
    tables = lax.dynamic_index_in_dim(jnp.asarray(table), own.astype(jnp.uint32), 0, False)
    entries = groups + 1

    flat_routes = routes.reshape(-1)
    hits = (flat_routes[:, None] == jnp.arange(experts, dtype=jnp.int32)).astype(BF16)
    earlier = jnp.tril(jnp.ones((2 * tok, 2 * tok), BF16), -1)
    ranks = jnp.sum(dot(earlier, hits, 1, 0) * hits.astype(F32), axis=1).astype(jnp.int32)
    slot = (flat_routes * capacity + ranks).reshape(tok, 2)
    ids = jnp.arange(experts * capacity, dtype=jnp.int32)
    pick = [(slot[:, k][:, None] == ids[None, :]).astype(BF16) for k in range(2)]
    either = pick[0] + pick[1]

    def dispatch(token_rows):
        slots = dot(either, token_rows, 0, 0).astype(BF16).reshape(devices, share, width)
        return to_all(slots).reshape(-1, width)

    def both_halves(value):
        other = lax.ppermute(value, "sc", SWAP)
        return jnp.concatenate([value, other], axis=0)

    cot_rows = both_halves(dispatch(cotangent))

    normed_group = (group_x * lax.rsqrt(jnp.mean(group_x * group_x, axis=-1, keepdims=True) + NORM_EPS) * gain1).astype(BF16)
    joined = jnp.concatenate([qkv_weight[0], qkv_weight[1], qkv_weight[2]], axis=1)
    projected = dot(joined, normed_group, 0, 1).astype(BF16)
    q_t = projected[:columns] * BF16(HD ** (-0.5))
    kv_own = projected[columns:]
    kvs = ring_gather(kv_own, ring)
    state = attend(tables, entries, 0, q_t, [kv_own, kv_own], lines, None, False, 1)
    for call_at in range(1, groups // 2 + 1):
        at = 2 * call_at - 1
        state = attend(tables, entries, at + 1, q_t, kvs[at : at + 2], lines, state, call_at == groups // 2)
    attn_t, lse = state

    def swap_weights(weight):
        kept, sent = jnp.where(is_x, weight[1], weight[0]), jnp.where(is_x, weight[0], weight[1])
        return kept, lax.ppermute(sent, "sx", SWAP)

    ups, downs = swap_weights(after(expert_up, kv_own)), swap_weights(after(expert_down, kv_own))
    router = gather_shard(router_weight, is_x, is_c).reshape(width, experts)
    grad_acts = []
    for part in range(2):
        grad_acts.append(dot(cot_rows, downs[part], 1, 1).astype(BF16))
    q_ext = jnp.concatenate([q_t, pack_rows(-lse[:heads])], axis=0)
    qs = ring_gather(q_ext, ring)

    x_own = layer_input.astype(F32)
    hidden = x_own + scatter_shard(dot(attn_t, out_weight, 0, 0), is_x, is_c)

    inverse2 = lax.rsqrt(jnp.mean(hidden * hidden, axis=-1, keepdims=True) + NORM_EPS)
    unit2 = hidden * inverse2
    normed2 = (unit2 * gain2).astype(BF16)
    probs = jax.nn.softmax(dot(normed2, router, 1, 0), axis=-1)
    chosen = [(routes[:, k : k + 1] == jnp.arange(experts, dtype=jnp.int32)[None, :]) for k in range(2)]
    gates = [jnp.sum(jnp.where(chosen[k], probs, 0.0), axis=1, keepdims=True) for k in range(2)]
    x_own_rows = dispatch(normed2)
    x_other_rows = lax.ppermute(x_own_rows, "sc", SWAP)
    mine = (2 * own + sx).astype(jnp.int32).reshape(1)
    front = expert_front(mine, x_own_rows, x_other_rows, ups, grad_acts, router)
    acts, grad_inners = front[:2], front[2:4]
    back, stats = front[4], front[6]
    got = lax.ppermute(front[5], "sc", SWAP).astype(F32)
    gate_sum = back[:, width : width + 1] + got[:, width : width + 1] + got[:, width + 1 : width + 2]
    high = lax.reduce_precision(gate_sum, 8, 7)
    lane = jnp.arange(128, dtype=jnp.int32)[None, :]
    gate_pair = jnp.where(lane == 0, high, jnp.where(lane == 1, gate_sum - high, 0.0))
    joined_back = jnp.concatenate([back[:, :width] + got[:, :width], gate_pair], axis=1).astype(BF16)
    grad_returned = to_all(joined_back.reshape(devices, share, width + 128)).reshape(-1, width + 128)

    count = x_own_rows.shape[0]
    x_rows = jnp.concatenate([x_own_rows, x_other_rows], axis=0)
    grad_rows = (stats[:, :1] * cot_rows.astype(F32)).astype(BF16)
    parts = dot(acts[0], downs[0], 1, 0) + dot(acts[1], downs[1], 1, 0)
    produced = (parts[:count] + lax.ppermute(parts[count:].astype(BF16), "sc", SWAP).astype(F32)).astype(BF16)
    sent_up = dot(x_rows, grad_inners[1], 0, 0).astype(BF16)
    sent_down = dot(acts[1], grad_rows, 0, 0).astype(BF16)
    returned = to_all(after(produced, grad_returned).reshape(devices, share, width)).reshape(-1, width)

    upstream = cotangent.astype(F32)
    taken = [dot(pick[k], grad_returned, 1, 0) for k in range(2)]
    grad_gate = [t[:, width : width + 1] + t[:, width + 1 : width + 2] for t in taken]
    grad_probs = jnp.where(chosen[0], grad_gate[0], 0.0) + jnp.where(chosen[1], grad_gate[1], 0.0)
    grad_logits = (probs * (grad_probs - jnp.sum(probs * grad_probs, axis=-1, keepdims=True))).astype(BF16)
    grad_normed2 = dot(grad_logits, router, 1, 1) + taken[0][:, :width] + taken[1][:, :width]
    scaled2 = gain2 * grad_normed2
    grad_hidden = upstream + inverse2 * (scaled2 - unit2 * jnp.mean(scaled2 * unit2, axis=-1, keepdims=True))

    grad_group = gather_shard(grad_hidden.astype(BF16), is_x, is_c).reshape(rows, width)
    do_t = dot(out_weight, grad_group, 1, 1).astype(BF16)
    delta = jnp.sum((do_t.astype(F32) * attn_t.astype(F32)).reshape(heads, HD, rows), axis=1)
    do_ext = jnp.concatenate([do_t, pack_rows(-delta)], axis=0)
    dos = ring_gather(do_ext, ring)
    state = key_side(tables, entries, 0, kv_own, [q_ext] * 2, [do_ext] * 2, lines, None, False, 1)
    for call_at in range(1, groups // 2 + 1):
        at = 2 * call_at - 1
        state = key_side(tables, entries, at + 1, kv_own, qs[at : at + 2], dos[at : at + 2], lines, state, call_at == groups // 2)
    grad_k, grad_v = state

    output = hidden + sum(gates[k] * dot(pick[k], returned, 1, 0) for k in range(2))

    cut = groups // 2 + 1
    do_query = after(do_ext, grad_k)
    kv_entries = [kv_own] + kvs
    state, diag_a = query_side(tables, entries, 0, q_ext, do_query, kv_entries[:cut], turned_lines, None, False, 1)
    grad_q, diag_b = query_side(tables, entries, cut, q_ext, do_query, kv_entries[cut:], turned_lines, state, True)

    signed = np.where(place < half, place, place - 2 * half)
    spans = jnp.asarray(bucket_numbers(np.arange(tiles)[:, None] * half - signed[None, :]))
    diagonals = jnp.concatenate([diag_a, diag_b], axis=1)
    at_tile = tables[4 * entries : 6 * entries].reshape(entries, 2).T
    used = (at_tile[..., None] == jnp.arange(tiles, dtype=jnp.int32)).astype(F32)
    by_tile = jnp.einsum("pet,pehc->thc", used, diagonals, precision=lax.Precision.HIGHEST)
    hot = (spans[..., None] == names).astype(F32)
    grad_table = jnp.einsum("thc,tck->kh", by_tile, hot, precision=lax.Precision.HIGHEST)

    def scatter_ctx(value):
        pieces = to_all(value.reshape((groups, value.shape[0] // groups) + value.shape[1:]), "ctx")
        return jnp.sum(pieces.astype(F32), axis=0).astype(BF16)

    def spread_ctx(piece):
        return to_all(jnp.broadcast_to(piece[None], (groups,) + piece.shape), "ctx").reshape((-1,) + piece.shape[1:])

    early = jnp.concatenate([dot(normed_group, grad_k, 0, 0), dot(normed_group, grad_v, 0, 0), dot(grad_group, attn_t, 0, 1)], axis=1)
    early_piece = scatter_ctx(after(early.astype(BF16), returned))
    late = dot(normed_group, grad_q, 0, 0).astype(BF16)
    late_piece = scatter_ctx(after(late, early_piece))
    late_all = spread_ctx(late_piece)
    slot_of = (jnp.arange(groups, dtype=jnp.int32)[:, None] == tables[6 * 2 * entries :][None, :]).astype(BF16)
    early_slots = jnp.stack(ring_gather(early_piece, ring))
    early_all = lax.dot_general(slot_of, early_slots, (((1,), (0,)), ((), ())), preferred_element_type=F32).reshape(width, 3 * columns)
    qkv_sum = jnp.stack([late_all.astype(F32), early_all[:, :columns], early_all[:, columns : 2 * columns]])
    out_sum = early_all[:, 2 * columns :].T

    def owners(kept, sent):
        got = lax.ppermute(after(sent, do_ext), "sx", SWAP)
        got = after(got, late_piece).astype(F32)
        return jnp.stack([jnp.where(is_x, got, kept), jnp.where(is_x, kept, got)])

    kept_up = dot(after(x_rows, grad_q), grad_inners[0], 0, 0)
    kept_down = dot(after(acts[0], grad_q), grad_rows, 0, 0)
    grad_up_own, grad_down_own = owners(kept_up, sent_up), owners(kept_down, sent_down)

    grad_joined = jnp.concatenate([grad_q, grad_k, grad_v], axis=1)
    partial = dot(grad_joined, joined, 1, 1)
    group_unit = group_x * lax.rsqrt(jnp.mean(group_x * group_x, axis=-1, keepdims=True) + NORM_EPS)
    grad_gain1 = jnp.sum(partial * group_unit, axis=0)
    grad_gain2 = jnp.sum(grad_normed2 * unit2, axis=0)
    small = jnp.concatenate([dot(grad_logits, normed2, 0, 0), grad_gain1[None], grad_gain2[None]], axis=0)
    small = small.reshape(experts + 2, 4, quarter).transpose(1, 0, 2)
    flat = jnp.concatenate([grad_table.reshape(-1), jnp.zeros((quarter - buckets * heads,), F32)])
    at_own = jnp.arange(4, dtype=jnp.int32) == 2 * sx + sc
    extra = jnp.where(at_own[:, None, None], flat[None, None, :], 0.0)
    small = jnp.concatenate([small, extra, jnp.zeros((4, -(experts + 3) % 16, quarter), F32)], axis=1)
    extra_rows = small.shape[1] * quarter // width
    mixed = jnp.concatenate([partial.reshape(4, tok, width), small.reshape(4, extra_rows, width)], axis=1)
    mixed = scatter_shard(mixed.reshape(-1, width), is_x, is_c)
    grad_normed1 = mixed[:tok]
    inverse1 = lax.rsqrt(jnp.mean(x_own * x_own, axis=-1, keepdims=True) + NORM_EPS)
    unit1 = x_own * inverse1
    scaled1 = gain1 * grad_normed1
    input_gradient = grad_hidden + inverse1 * (scaled1 - unit1 * jnp.mean(scaled1 * unit1, axis=-1, keepdims=True))
    small = sum(s.astype(F32) for s in ring_gather(mixed[tok:].astype(BF16), ring)).reshape(-1, quarter)
    table_sum = small[experts + 2, : buckets * heads].reshape(buckets, heads)
    return (output, input_gradient, small[experts], qkv_sum, table_sum, out_sum, small[experts + 1],
            small[:experts].T, grad_up_own, grad_down_own)


def solution(mesh):
    ctx, shard = mesh.shape["ctx"], mesh.shape["shard"]
    inner = jax.sharding.Mesh(mesh.devices.reshape(ctx, shard // 2, 2), ALL)
    ring = ring_of(ctx)
    tokens = P(ALL, None)
    in_specs = (tokens, P(SHARD), P(None, None, SHARD), P(None, SHARD), P(SHARD, None), P(SHARD), P(SHARD, None),
                P("ctx", None, SHARD), P("ctx", SHARD, None), tokens, tokens)
    out_specs = (tokens, tokens, P(SHARD), P(None, None, SHARD), P(None, SHARD), P(SHARD, None), P(SHARD),
                 P(SHARD, None), P("ctx", None, SHARD), P("ctx", SHARD, None))

    def step(layer_input, *args):
        half = 2 * layer_input.shape[0]
        return body(ring, entry_tables(ring, tile_count(ctx, half)), layer_input, *args)

    return jax.shard_map(step, mesh=inner, in_specs=in_specs, out_specs=out_specs, check_vma=False)
```

```python
import functools

import jax
import numpy as np
import jax.numpy as jnp
from jax import lax
from jax.experimental import pallas as pl
from jax.sharding import PartitionSpec as P
from jax.experimental.pallas import tpu as pltpu

HD = 64
STATS = 16
MASKED = -1e30
F32 = jnp.float32
BF16 = jnp.bfloat16


def nn(a, b):
    return lax.dot_general(a, b, (((1,), (0,)), ((), ())), preferred_element_type=F32)


def nt(a, b):
    return lax.dot_general(a, b, (((1,), (1,)), ((), ())), preferred_element_type=F32)


def bias_of(line_ref, tile, head):
    width = line_ref.shape[2]
    half = width // 2
    base = jnp.broadcast_to(line_ref[tile, head : head + 1, :], (8, width))
    base = pltpu.roll(base, 0, 1, stride=1, stride_axis=0)
    moved = [pltpu.roll(base, (half + 1 + 8 * b) % width, 1) for b in range(128 // 8)]
    pieces = []
    for over in range(half // 128):
        cut = 128 * over
        for m in moved:
            pieces.append(jnp.concatenate([m[:, width - cut :], m[:, : half - cut]], axis=1) if over else m[:, :half])
    return jnp.concatenate(pieces, axis=0)


def to_heads(feature_major, dst, heads, extra=None):
    count, rows = feature_major.shape
    padded = jnp.concatenate([feature_major.astype(F32), jnp.zeros((-count % 128, rows), F32)], axis=0)
    natural = jnp.transpose(padded).astype(BF16)
    columns = heads * HD
    for h in range(heads):
        dst[h, :, :HD] = natural[:, HD * h : HD * h + HD]
        if extra is not None:
            dst[h, :, HD:] = natural[:, columns : columns + STATS] if extra == "stats" else picks(h, heads, (rows, STATS), 1)


def picks(head, heads, shape, axis):
    at = lax.broadcasted_iota(jnp.int32, shape, axis)
    return jnp.where((at % heads == head) & (at < 3 * heads), 1.0, 0.0).astype(BF16)


def pack_rows(values):
    high = lax.reduce_precision(values, 8, 7)
    rest = values - high
    mid = lax.reduce_precision(rest, 8, 7)
    low = rest - mid
    blank = jnp.zeros((STATS - 3 * values.shape[0], values.shape[1]), BF16)
    return jnp.concatenate([high.astype(BF16), mid.astype(BF16), low.astype(BF16), blank], axis=0)


HELD = pl.BlockSpec(memory_space=pltpu.VMEM)
TABLE = pl.BlockSpec(memory_space=pltpu.SMEM)
PARAMS = pltpu.CompilerParams(vmem_limit_bytes=24 << 20)


def entry_at(entries, side, kind, entry, step):
    return ((side * 3 + kind) * entries + entry) * 2 + step


def in_steps(count, alone, heads, begin, finish):
    def one(step, nothing):
        items = [(e, h) for e in range(count) if e != alone for h in range(heads)]
        following = begin(step, *items[0])
        for number, item in enumerate(items):
            current = following
            if number + 1 < len(items):
                following = begin(step, *items[number + 1])
            finish(step, *item, *current)
        return nothing

    lax.fori_loop(0, 2, one, 0)
    if 0 <= alone:
        for h in range(heads):
            finish(0, alone, h, *begin(0, alone, h))


def columns_at(ref, begin, count, at, half):
    return ref[begin : begin + count, pl.ds(pl.multiple_of(at * half, half), half)]


def forward_kernel(at, count, alone, first, last, tab, q_ref, *refs):
    kv_refs, line_ref, refs = refs[:count], refs[count], refs[count + 1 :]
    if not first:
        before_ref, refs = refs[0], refs[1:]
    if last:
        out_ref, lse_ref, k_nat, state = refs
    else:
        state, k_nat = refs
    heads, half = line_ref.shape[1], line_ref.shape[2] // 2
    columns = heads * HD

    for e in range(count):
        if e != alone:
            to_heads(kv_refs[e][:columns, :], k_nat.at[e], heads)
    if first:
        state[...] = jnp.zeros(state.shape, F32)
        for h in range(heads):
            state[h, HD + STATS :, :] = jnp.full((8, state.shape[2]), MASKED, F32)
    else:
        state[...] = before_ref[...]

    ones = jnp.ones((STATS, half), BF16)

    def spots(step, e):
        lanes = pl.ds(pl.multiple_of(tab[at(0, e, step)] * half, half), half)
        return lanes, tab[at(1, e, step)], tab[at(2, e, step)]

    def begin(step, e, h):
        lanes, side, _ = spots(step, e)
        rows = pl.ds(pl.multiple_of(side * half, half), half)
        return (nn(k_nat[0 if e == alone else e, h, rows, :], q_ref[HD * h : HD * h + HD, lanes]),)

    def finish(step, e, h, s):
        lanes, side, tile = spots(step, e)
        s = s + bias_of(line_ref, tile, h)
        m_old = state[h, HD + STATS : HD + STATS + 1, lanes]
        m_new = jnp.maximum(m_old, jnp.max(s, axis=0, keepdims=True))
        p = jnp.exp(s - m_new)
        v_ext = jnp.concatenate([columns_at(kv_refs[e], columns + HD * h, HD, side, half), ones], axis=0)
        kept = state[h, : HD + STATS, lanes] * jnp.exp(m_old - m_new)
        state[h, : HD + STATS, lanes] = kept + nn(v_ext, p.astype(BF16))
        state[h, HD + STATS :, lanes] = jnp.broadcast_to(m_new, (8, half))

    in_steps(count, alone, heads, begin, finish)

    if last:
        for h in range(heads):
            total = state[h, HD : HD + 1, :]
            out_ref[HD * h : HD * h + HD, :] = (state[h, :HD, :] / total).astype(BF16)
            lse_ref[h : h + 1, :] = state[h, HD + STATS : HD + STATS + 1, :] + jnp.log(total)


def call(kernel, out_shape, scratch, *operands):
    many = isinstance(out_shape, list)
    return pl.pallas_call(
        kernel, out_shape=out_shape, out_specs=[HELD] * len(out_shape) if many else HELD,
        in_specs=[TABLE] + [HELD] * (len(operands) - 1), scratch_shapes=scratch, compiler_params=PARAMS,
    )(*operands)


def attend(tab, entries, begin, q_t, kvs, lines, state, last, alone=-1):
    at = lambda kind, e, p: entry_at(entries, 0, kind, begin + e, p)
    heads = lines.shape[1]
    columns, rows = q_t.shape
    kind = (heads, HD + STATS + 8, rows)
    first = state is None
    scratch = [pltpu.VMEM((len(kvs), heads, rows, HD), BF16)] + ([pltpu.VMEM(kind, F32)] if last else [])
    finished = [jax.ShapeDtypeStruct((columns, rows), BF16), jax.ShapeDtypeStruct((8, rows), F32)]
    return call(
        lambda *refs: forward_kernel(at, len(kvs), alone, first, last, *refs),
        finished if last else jax.ShapeDtypeStruct(kind, F32), scratch,
        tab, q_t, *kvs, lines, *(() if first else (state,)))


def query_kernel(at, count, alone, first, last, tab, q_ref, do_ref, *refs):
    kv_refs, line_ref, refs = refs[:count], refs[count], refs[count + 1 :]
    if not first:
        before_ref, refs = refs[0], refs[1:]
    out_ref, diag_ref, q_nat, do_nat = refs[:4]
    acc = refs[4] if last else out_ref
    heads, half = line_ref.shape[1], line_ref.shape[2] // 2
    columns = heads * HD

    to_heads(q_ref[...], q_nat, heads, "stats")
    to_heads(do_ref[...], do_nat, heads, "stats")
    if first:
        acc[...] = jnp.zeros(acc.shape, F32)
    else:
        acc[...] = before_ref[...]

    line = lax.broadcasted_iota(jnp.int32, (8, 2 * half), 0)
    blank = jnp.zeros((8, half), F32)
    chosen = [picks(h, heads, (STATS, half), 0) for h in range(heads)]

    if 0 <= alone:
        diag_ref[1, alone] = jnp.zeros(diag_ref.shape[2:], F32)

    def spots(step, e, h):
        side = tab[at(1, e, step)]
        k_t = columns_at(kv_refs[e], HD * h, HD, side, half)
        v_t = columns_at(kv_refs[e], columns + HD * h, HD, side, half)
        return pl.ds(pl.multiple_of(tab[at(0, e, step)] * half, half), half), k_t, v_t

    def begin(step, e, h):
        rows, k_t, v_t = spots(step, e, h)
        return (nn(q_nat[h, rows, :], jnp.concatenate([k_t, chosen[h]], axis=0)),
                nn(do_nat[h, rows, :], jnp.concatenate([v_t, chosen[h]], axis=0)))

    def finish(step, e, h, s, dp):
        rows, k_t, _ = spots(step, e, h)
        ds = jnp.exp(s + bias_of(line_ref, tab[at(2, e, step)], h)) * dp
        acc[h, rows, :] += nt(ds.astype(BF16), k_t)
        total = jnp.zeros((8, 2 * half), F32)
        for b in range(128 // 8):
            piece = jnp.concatenate([ds[8 * b : 8 * b + 8, :], blank], axis=1)
            for over in range(1, half // 128):
                cut = 128 * over
                moved = ds[cut + 8 * b : cut + 8 * b + 8, :]
                piece = piece + jnp.concatenate([moved[:, cut:], blank, moved[:, :cut]], axis=1)
            total = total + (pltpu.roll(piece, 2 * half - 8 * b, 1) if b else piece)
        for bit in (1, 2, 4):
            total = jnp.where((line & bit) != 0, pltpu.roll(total, 2 * half - bit, 1), total)
        diag_ref[step, e, h : h + 1, :] = jnp.sum(total, axis=0, keepdims=True)

    in_steps(count, alone, heads, begin, finish)

    if last:
        out_ref[...] = jnp.concatenate([acc[h] * HD ** (-0.5) for h in range(heads)], axis=1).astype(BF16)


def query_side(tab, entries, begin, q_ext, do_ext, kvs, lines, state, last, alone=-1):
    at = lambda kind, e, p: entry_at(entries, 0, kind, begin + e, p)
    heads, width = lines.shape[1], lines.shape[2]
    extended, rows = q_ext.shape
    kind = (heads, rows, HD)
    first = state is None
    scratch = [pltpu.VMEM((heads, rows, HD + STATS), BF16)] * 2
    out_kind = ((rows, extended - STATS), BF16) if last else (kind, F32)
    return call(
        lambda *refs: query_kernel(at, len(kvs), alone, first, last, *refs),
        [jax.ShapeDtypeStruct(*out_kind), jax.ShapeDtypeStruct((2, len(kvs), heads, width), F32)],
        scratch + ([pltpu.VMEM(kind, F32)] if last else []),
        tab, q_ext, do_ext, *kvs, lines, *(() if first else (state,)))


def key_kernel(at, count, alone, first, last, tab, kv_ref, *refs):
    q_refs, do_refs, line_ref, refs = refs[:count], refs[count : 2 * count], refs[2 * count], refs[2 * count + 1 :]
    if not first:
        before_ref, refs = refs[0], refs[1:]
    if last:
        dk_ref, dv_ref, k_nat, v_nat, state = refs
    else:
        state, k_nat, v_nat = refs
    heads, half = line_ref.shape[1], line_ref.shape[2] // 2
    columns = heads * HD

    to_heads(kv_ref[:columns, :], k_nat, heads, "picks")
    to_heads(kv_ref[columns:, :], v_nat, heads, "picks")
    if first:
        state[...] = jnp.zeros(state.shape, F32)
    else:
        state[...] = before_ref[...]

    def do(e, step):
        rows = pl.ds(pl.multiple_of(tab[at(0, e, step)] * half, half), half)
        q_ref, do_ref, side, tile = q_refs[e], do_refs[e], tab[at(1, e, step)], tab[at(2, e, step)]
        lse, delta = columns_at(q_ref, columns, STATS, side, half), columns_at(do_ref, columns, STATS, side, half)
        for h in range(heads):
            q_t = columns_at(q_ref, HD * h, HD, side, half)
            do_t = columns_at(do_ref, HD * h, HD, side, half)
            p = jnp.exp(nn(k_nat[h, rows, :], jnp.concatenate([q_t, lse], axis=0)) + bias_of(line_ref, tile, h))
            state[1, h, rows, :] += nt(p.astype(BF16), do_t)
            ds = p * nn(v_nat[h, rows, :], jnp.concatenate([do_t, delta], axis=0))
            state[0, h, rows, :] += nt(ds.astype(BF16), q_t)

    def one(step, nothing):
        for e in range(count):
            if e != alone:
                do(e, step)
        return nothing

    lax.fori_loop(0, 2, one, 0)
    if 0 <= alone:
        do(alone, 0)

    if last:
        dk_ref[...] = jnp.concatenate([state[0, h] for h in range(heads)], axis=1).astype(BF16)
        dv_ref[...] = jnp.concatenate([state[1, h] for h in range(heads)], axis=1).astype(BF16)


def key_side(tab, entries, begin, kv_own, qs, dos, lines, state, last, alone=-1):
    at = lambda kind, e, p: entry_at(entries, 1, kind, begin + e, p)
    heads = lines.shape[1]
    columns, rows = kv_own.shape[0] // 2, kv_own.shape[1]
    kind = (2, heads, rows, HD)
    first = state is None
    finished = [jax.ShapeDtypeStruct((rows, columns), BF16)] * 2
    return call(
        lambda *refs: key_kernel(at, len(qs), alone, first, last, *refs),
        finished if last else jax.ShapeDtypeStruct(kind, F32),
        [pltpu.VMEM((heads, rows, HD + STATS), BF16)] * 2 + ([pltpu.VMEM(kind, F32)] if last else []),
        tab, kv_own, *qs, *dos, lines, *(() if first else (state,)))


CURVE = 0.7978845608028654


def expert_kernel(mine_ref, own_ref, other_ref, up_a, up_b, grad_a, grad_b, router_ref,
                  act_a, act_b, inner_a, inner_b, kept_ref, sent_ref, stats_ref, *, block, experts):
    count, width = own_ref.shape
    at_expert = lax.broadcasted_iota(jnp.int32, (block, router_ref.shape[1]), 1)
    at_lane = lax.broadcasted_iota(jnp.int32, (block, 128), 1)

    def one(tile, nothing, source, mine_here):
        place = pl.ds(pl.multiple_of(tile * block, block), block)
        rows = pl.ds(pl.multiple_of(tile * block + (0 if mine_here else count), block), block)
        x = source[place, :]
        logits = jnp.where(at_expert < experts, nn(x, router_ref[...]), MASKED)
        powers = jnp.exp(logits - jnp.max(logits, axis=1, keepdims=True))
        share = jnp.sum(jnp.where(at_expert == mine_ref[0], powers, 0.0), axis=1, keepdims=True)
        gate = share / jnp.sum(powers, axis=1, keepdims=True)
        back = jnp.zeros((block, width), F32)
        paid = jnp.zeros((block, 128), F32)
        steps = [(up, grads, act_ref, inner_ref, slice(cut, cut + 256))
                 for up, grads, act_ref, inner_ref in ((up_a, grad_a, act_a, inner_a), (up_b, grad_b, act_b, inner_b))
                 for cut in range(0, up.shape[1], 256)]
        following = nn(x, steps[0][0][:, steps[0][4]])
        for number, (up, grads, act_ref, inner_ref, piece) in enumerate(steps):
            u = following
            if number + 1 < len(steps):
                following = nn(x, steps[number + 1][0][:, steps[number + 1][4]])
            square = u * u
            t = jnp.tanh(u * (CURVE + (CURVE * 0.044715) * square))
            high = 0.5 + 0.5 * t
            act = (u * high).astype(BF16)
            act_ref[rows, piece] = act
            slope = high + u * (high * (1.0 - t)) * (CURVE + (CURVE * 0.134145) * square)
            g = grads[rows, piece].astype(F32)
            inner = (gate * (g * slope)).astype(BF16)
            inner_ref[rows, piece] = inner
            back = back + nt(inner, up[:, piece])
            product = act.astype(F32) * g
            paid = paid + product[:, :128] + product[:, 128:]
        paid = jnp.sum(paid, axis=1, keepdims=True)
        if mine_here:
            kept_ref[place, :width] = back
            kept_ref[place, width:] = jnp.where(at_lane == 0, paid, 0.0)
        else:
            high = paid.astype(BF16).astype(F32)
            sent_ref[place, :width] = back.astype(BF16)
            sent_ref[place, width:] = jnp.where(at_lane == 0, high, jnp.where(at_lane == 1, paid - high, 0.0)).astype(BF16)
        stats_ref[rows, :] = jnp.broadcast_to(gate, (block, 128))
        return nothing

    for source, mine_here in ((own_ref, True), (other_ref, False)):
        lax.fori_loop(0, count // block, functools.partial(one, source=source, mine_here=mine_here), 0)


def expert_front(mine, own, other, ups, grads, router, experts):
    count, width = own.shape
    hidden = ups[0].shape[1]
    rows = 2 * count
    wide = [jax.ShapeDtypeStruct((rows, hidden), BF16)] * 4
    return pl.pallas_call(
        lambda *refs: expert_kernel(*refs, block=256, experts=experts), name="expert_front",
        in_specs=[TABLE] + [HELD] * 7, out_specs=[HELD] * 7,
        out_shape=wide + [jax.ShapeDtypeStruct((count, width + 128), F32), jax.ShapeDtypeStruct((count, width + 128), BF16),
                          jax.ShapeDtypeStruct((rows, 128), F32)],
        compiler_params=pltpu.CompilerParams(vmem_limit_bytes=32 << 20),
    )(mine, own, other, *ups, *grads, router)


def place_kernel(at, tab, *refs):
    slots, out = refs[:-1], refs[-1]
    kinds, step = out.shape[0], slots[0].shape[0] // out.shape[0]
    for e, slot in enumerate(slots):
        rows = pl.ds(pl.multiple_of(tab[at + e] * step, step), step)
        for kind in range(kinds):
            out[kind, rows, :] = slot[kind * step : (kind + 1) * step, :].astype(F32)


def place_slots(slots, tab, at):
    count, width = slots[0].shape
    step = count // 3
    if step % 8:
        order = (jnp.arange(len(slots), dtype=jnp.int32)[:, None] == tab[at:][None, :]).astype(BF16)
        placed = lax.dot_general(order, jnp.stack(slots), (((1,), (0,)), ((), ())), preferred_element_type=F32)
        return placed.reshape(len(slots), 3, step, width).transpose(1, 0, 2, 3).reshape(3, -1, width)
    return call(lambda *refs: place_kernel(at, *refs), jax.ShapeDtypeStruct((3, len(slots) * step, width), F32), [], tab, *slots)


NORM_EPS = 1e-06
ALL = ("ctx", "sx", "sc")
SHARD = ("sx", "sc")
SWAP = ((0, 1), (1, 0))


def bucket_numbers(distance):
    square = np.maximum(distance, 0).astype(np.int64) ** 2
    counted = sum((square >= 256 << j).astype(np.int32) for j in range(1, 16))
    return np.where(distance < 16, np.maximum(distance, 0), 16 + counted).astype(np.int32)


def tile_count(groups, half):
    count = 2
    while count < 2 * groups and ((count - 1) * half - half + 1) ** 2 < 256 << 15:
        count += 1
    return count


def ring_of(size):
    return list(range(0, size, 2)) + list(range(size - 1, 0, -2))


def ring_steps(size):
    steps = []
    for hop in range(1, size // 2 + 1):
        steps.append(-hop)
        if hop < size // 2:
            steps.append(hop)
    return steps


def entry_tables(ring, tiles):
    size = len(ring)
    top = 2 * size - 1
    place = {g: i for i, g in enumerate(ring)}
    tables = []
    for own in range(size):
        query = [[(0, 0, 0), (1, 1, 0)], [(1, 0, top - 2 * own)] * 2]
        key = [[(0, 0, 0), (1, 1, 0)], [(0, 1, top - 2 * own)] * 2]
        for step in ring_steps(size):
            other = ring[(place[own] + step) % size]
            if other < own:
                query.append([(1, 0, top - own - other), (0, 0, own - other)])
                key.append([(0, 1, top - own - other), (1, 1, own - other)])
            else:
                query.append([(1, 0, top - own - other), (1, 1, other - own)])
                key.append([(0, 1, top - own - other), (0, 0, other - own)])
        tables.append([query, key])
    table = np.array(tables, np.int32).transpose(0, 1, 4, 2, 3)
    table[:, :, 2] = np.minimum(table[:, :, 2], tiles - 1)
    slots = [[own] + [ring[(place[own] + step) % size] for step in ring_steps(size)] for own in range(size)]
    return np.concatenate([table.reshape(size, -1), np.array(slots, np.int32)], axis=1)


def ring_gather(value, ring):
    size = len(ring)
    forth = [(ring[i], ring[(i + 1) % size]) for i in range(size)]
    back = [(b, a) for a, b in forth]
    slots, left, right = [value], value, value
    for hop in range(1, size // 2 + 1):
        left = lax.ppermute(left, "ctx", forth)
        slots.append(left)
        if hop < size // 2:
            right = lax.ppermute(right, "ctx", back)
            slots.append(right)
    return slots


def gather_shard(value, is_x, is_c):
    across = lax.ppermute(value, "sx", SWAP)
    pair = jnp.stack([jnp.where(is_x, across, value), jnp.where(is_x, value, across)])
    other = lax.ppermute(pair, "sc", SWAP)
    return jnp.stack([jnp.where(is_c, other, pair), jnp.where(is_c, pair, other)], axis=1).reshape((4,) + value.shape)


def scatter_shard(parts, is_x, is_c):
    split = parts.reshape((2, 2, parts.shape[0] // 4) + parts.shape[1:])
    kept, sent = jnp.where(is_c, split[:, 1], split[:, 0]), jnp.where(is_c, split[:, 0], split[:, 1])
    both = kept + lax.ppermute(sent.astype(BF16), "sc", SWAP).astype(F32)
    mine, theirs = jnp.where(is_x, both[1], both[0]), jnp.where(is_x, both[0], both[1])
    return mine + lax.ppermute(theirs.astype(BF16), "sx", SWAP).astype(F32)


def dot(a, b, ca, cb):
    return lax.dot_general(a, b, (((ca,), (cb,)), ((), ())), preferred_element_type=F32)


def to_all(value, axes=ALL):
    return lax.all_to_all(value, axes, split_axis=0, concat_axis=0, tiled=True)


def after(value, *others):
    return lax.optimization_barrier((value,) + others)[0]


def body(ring, table, layer_input, norm1_gain, qkv_weight, rel_bias, out_weight, norm2_gain, router_weight,
         expert_up, expert_down, routes, cotangent):
    groups = len(ring)
    own, sx, sc = lax.axis_index("ctx"), lax.axis_index("sx"), lax.axis_index("sc")
    is_x, is_c = sx == 1, sc == 1
    tok, width = layer_input.shape
    buckets, heads = rel_bias.shape
    columns = heads * HD
    experts = router_weight.shape[1]
    capacity = 4 * tok // experts
    rows = 4 * tok
    half = rows // 2
    quarter = norm1_gain.shape[0]
    devices = 2 * experts
    share = experts * capacity // devices

    group_x = gather_shard(layer_input, is_x, is_c).reshape(rows, width).astype(F32)
    gains = jnp.concatenate([norm1_gain.reshape(1, -1), norm2_gain.reshape(1, -1), jnp.zeros((14, quarter), BF16)], axis=0)
    gains = gather_shard(gains, is_x, is_c).astype(F32)
    gain1, gain2 = gains[:, 0].reshape(-1), gains[:, 1].reshape(-1)

    tiles = tile_count(groups, half)
    place = np.arange(2 * half)
    spread = np.arange(tiles)[:, None] * half + place[None, :] - half + 1
    numbers = bucket_numbers(spread)
    turned = (2 * half - 2 - place) % (2 * half)
    names = jnp.arange(buckets, dtype=jnp.int32)

    def line(ids, distances):
        hot = (jnp.asarray(ids)[..., None] == names).astype(F32)
        values = jnp.einsum("tck,kh->thc", hot, rel_bias, precision=lax.Precision.HIGHEST)
        return jnp.where(jnp.asarray(distances < 0)[:, None, :], MASKED, values)

    lines, turned_lines = line(numbers, spread), line(numbers[:, turned], spread[:, turned])
    tables = lax.dynamic_index_in_dim(jnp.asarray(table), own.astype(jnp.uint32), 0, False)
    entries = groups + 1

    flat_routes = routes.reshape(-1)
    hits = (flat_routes[:, None] == jnp.arange(experts, dtype=jnp.int32)).astype(BF16)
    earlier = jnp.tril(jnp.ones((2 * tok, 2 * tok), BF16), -1)
    ranks = jnp.sum(dot(earlier, hits, 1, 0) * hits.astype(F32), axis=1).astype(jnp.int32)
    slot = (flat_routes * capacity + ranks).reshape(tok, 2)
    ids = jnp.arange(experts * capacity, dtype=jnp.int32)
    pick = [(slot[:, k][:, None] == ids[None, :]).astype(BF16) for k in range(2)]
    either = pick[0] + pick[1]

    def dispatch(token_rows):
        slots = dot(either, token_rows, 0, 0).astype(BF16).reshape(devices, share, width)
        return to_all(slots).reshape(-1, width)

    def both_halves(value):
        other = lax.ppermute(value, "sc", SWAP)
        return jnp.concatenate([value, other], axis=0)

    cot_rows = both_halves(dispatch(cotangent))

    normed_group = (group_x * lax.rsqrt(jnp.mean(group_x * group_x, axis=-1, keepdims=True) + NORM_EPS) * gain1).astype(BF16)
    joined = jnp.concatenate([qkv_weight[0], qkv_weight[1], qkv_weight[2]], axis=1)
    projected = dot(joined, normed_group, 0, 1).astype(BF16)
    q_t = projected[:columns] * BF16(HD ** (-0.5))
    kv_own = projected[columns:]
    kvs = ring_gather(kv_own, ring)
    state = attend(tables, entries, 0, q_t, [kv_own, kv_own], lines, None, False, 1)
    for call_at in range(1, groups // 2 + 1):
        at = 2 * call_at - 1
        state = attend(tables, entries, at + 1, q_t, kvs[at : at + 2], lines, state, call_at == groups // 2)
    attn_t, lse = state

    def swap_weights(weight):
        kept, sent = jnp.where(is_x, weight[1], weight[0]), jnp.where(is_x, weight[0], weight[1])
        return kept, lax.ppermute(sent, "sx", SWAP)

    ups, downs = swap_weights(after(expert_up, kv_own)), swap_weights(after(expert_down, kv_own))
    router = gather_shard(router_weight, is_x, is_c).reshape(width, experts)
    padded_router = jnp.concatenate([router, jnp.zeros((width, -experts % 128), BF16)], axis=1)
    grad_acts = []
    for part in range(2):
        grad_acts.append(dot(cot_rows, downs[part], 1, 1).astype(BF16))
    q_ext = jnp.concatenate([q_t, pack_rows(-lse[:heads])], axis=0)
    qs = ring_gather(q_ext, ring)

    x_own = layer_input.astype(F32)
    hidden = x_own + scatter_shard(dot(attn_t, out_weight, 0, 0), is_x, is_c)

    inverse2 = lax.rsqrt(jnp.mean(hidden * hidden, axis=-1, keepdims=True) + NORM_EPS)
    unit2 = hidden * inverse2
    normed2 = (unit2 * gain2).astype(BF16)
    probs = jax.nn.softmax(dot(normed2, router, 1, 0), axis=-1)
    chosen = [(routes[:, k : k + 1] == jnp.arange(experts, dtype=jnp.int32)[None, :]) for k in range(2)]
    gates = [jnp.sum(jnp.where(chosen[k], probs, 0.0), axis=1, keepdims=True) for k in range(2)]
    x_own_rows = dispatch(after(normed2, padded_router))
    x_other_rows = lax.ppermute(x_own_rows, "sc", SWAP)
    mine = (2 * own + sx).astype(jnp.int32).reshape(1)
    front = expert_front(mine, x_own_rows, x_other_rows, ups, grad_acts, padded_router, experts)
    acts, grad_inners = front[:2], front[2:4]
    back, stats = front[4], front[6]
    got = lax.ppermute(front[5], "sc", SWAP).astype(F32)
    gate_sum = back[:, width : width + 1] + got[:, width : width + 1] + got[:, width + 1 : width + 2]
    high = lax.reduce_precision(gate_sum, 8, 7)
    lane = jnp.arange(128, dtype=jnp.int32)[None, :]
    gate_pair = jnp.where(lane == 0, high, jnp.where(lane == 1, gate_sum - high, 0.0))
    joined_back = jnp.concatenate([back[:, :width] + got[:, :width], gate_pair], axis=1).astype(BF16)
    grad_returned = to_all(joined_back.reshape(devices, share, width + 128)).reshape(-1, width + 128)

    count = x_own_rows.shape[0]
    x_rows = jnp.concatenate([x_own_rows, x_other_rows], axis=0)
    grad_rows = (stats[:, :1] * cot_rows.astype(F32)).astype(BF16)
    parts = dot(acts[0], downs[0], 1, 0) + dot(acts[1], downs[1], 1, 0)
    produced = (parts[:count] + lax.ppermute(parts[count:].astype(BF16), "sc", SWAP).astype(F32)).astype(BF16)
    sent_up = dot(x_rows, grad_inners[1], 0, 0).astype(BF16)
    sent_down = dot(acts[1], grad_rows, 0, 0).astype(BF16)
    kept_up = dot(x_rows, grad_inners[0], 0, 0)
    kept_down = dot(acts[0], grad_rows, 0, 0)
    returned = to_all(after(produced, grad_returned).reshape(devices, share, width)).reshape(-1, width)

    upstream = cotangent.astype(F32)
    taken = [dot(pick[k], grad_returned, 1, 0) for k in range(2)]
    grad_gate = [t[:, width : width + 1] + t[:, width + 1 : width + 2] for t in taken]
    grad_probs = jnp.where(chosen[0], grad_gate[0], 0.0) + jnp.where(chosen[1], grad_gate[1], 0.0)
    grad_logits = (probs * (grad_probs - jnp.sum(probs * grad_probs, axis=-1, keepdims=True))).astype(BF16)
    grad_normed2 = dot(grad_logits, router, 1, 1) + taken[0][:, :width] + taken[1][:, :width]
    scaled2 = gain2 * grad_normed2
    grad_hidden = upstream + inverse2 * (scaled2 - unit2 * jnp.mean(scaled2 * unit2, axis=-1, keepdims=True))

    grad_group = gather_shard(grad_hidden.astype(BF16), is_x, is_c).reshape(rows, width)
    do_t = dot(out_weight, grad_group, 1, 1).astype(BF16)
    delta = jnp.sum((do_t.astype(F32) * attn_t.astype(F32)).reshape(heads, HD, rows), axis=1)
    do_ext = jnp.concatenate([do_t, pack_rows(-delta)], axis=0)
    dos = ring_gather(do_ext, ring)
    state = key_side(tables, entries, 0, kv_own, [q_ext] * 2, [do_ext] * 2, lines, None, False, 1)
    for call_at in range(1, groups // 2 + 1):
        at = 2 * call_at - 1
        state = key_side(tables, entries, at + 1, kv_own, qs[at : at + 2], dos[at : at + 2], lines, state, call_at == groups // 2)
    grad_k, grad_v = state

    output = hidden + sum(gates[k] * dot(pick[k], returned, 1, 0) for k in range(2))

    cut = groups // 2 + 1
    do_query = after(do_ext, grad_k)
    kv_entries = [kv_own] + kvs
    state, diag_a = query_side(tables, entries, 0, q_ext, do_query, kv_entries[:cut], turned_lines, None, False, 1)
    grad_q, diag_b = query_side(tables, entries, cut, q_ext, do_query, kv_entries[cut:], turned_lines, state, True)

    signed = np.where(place < half, place, place - 2 * half)
    spans = jnp.asarray(bucket_numbers(np.arange(tiles)[:, None] * half - signed[None, :]))
    diagonals = jnp.concatenate([diag_a, diag_b], axis=1)
    at_tile = tables[4 * entries : 6 * entries].reshape(entries, 2).T
    used = (at_tile[..., None] == jnp.arange(tiles, dtype=jnp.int32)).astype(F32)
    by_tile = jnp.einsum("pet,pehc->thc", used, diagonals, precision=lax.Precision.HIGHEST)
    hot = (spans[..., None] == names).astype(F32)
    grad_table = jnp.einsum("thc,tck->kh", by_tile, hot, precision=lax.Precision.HIGHEST)

    def scatter_ctx(value):
        pieces = to_all(value, "ctx")
        return pieces, jnp.sum(pieces.astype(F32), axis=0).astype(BF16)

    def chunks(value):
        return value.astype(BF16).reshape((groups, -1) + value.shape[1:])

    early = jnp.concatenate([chunks(dot(grad_k, normed_group, 0, 0)), chunks(dot(grad_v, normed_group, 0, 0)), chunks(dot(attn_t, grad_group, 1, 0))], axis=1)
    early_pieces, early_piece = scatter_ctx(after(early, returned))
    late = chunks(dot(grad_q, normed_group, 0, 0))
    late_pieces, late_piece = scatter_ctx(after(late, early_pieces))
    early_slots = ring_gather(early_piece, ring)

    def owners(kept, sent):
        got = lax.ppermute(after(sent, do_ext), "sx", SWAP)
        got = after(got, late_pieces).astype(F32)
        return jnp.stack([jnp.where(is_x, got, kept), jnp.where(is_x, kept, got)])

    grad_up_own, grad_down_own = owners(kept_up, sent_up), owners(kept_down, sent_down)

    grad_joined = jnp.concatenate([grad_q, grad_k, grad_v], axis=1)
    partial = dot(grad_joined, joined, 1, 1)
    group_unit = group_x * lax.rsqrt(jnp.mean(group_x * group_x, axis=-1, keepdims=True) + NORM_EPS)
    grad_gain1 = jnp.sum(partial * group_unit, axis=0)
    grad_gain2 = jnp.sum(grad_normed2 * unit2, axis=0)
    small = jnp.concatenate([dot(grad_logits, normed2, 0, 0), grad_gain1[None], grad_gain2[None]], axis=0)
    small = small.reshape(experts + 2, 4, quarter).transpose(1, 0, 2)
    flat = jnp.concatenate([grad_table.reshape(-1), jnp.zeros((quarter - buckets * heads,), F32)])
    at_own = jnp.arange(4, dtype=jnp.int32) == 2 * sx + sc
    extra = jnp.where(at_own[:, None, None], flat[None, None, :], 0.0)
    small = jnp.concatenate([small, extra, jnp.zeros((4, -(experts + 3) % 16, quarter), F32)], axis=1)
    extra_rows = small.shape[1] * quarter // width
    mixed = jnp.concatenate([partial.reshape(4, tok, width), small.reshape(4, extra_rows, width)], axis=1)
    mixed = scatter_shard(mixed.reshape(-1, width), is_x, is_c)
    grad_normed1 = mixed[:tok]
    inverse1 = lax.rsqrt(jnp.mean(x_own * x_own, axis=-1, keepdims=True) + NORM_EPS)
    unit1 = x_own * inverse1
    scaled1 = gain1 * grad_normed1
    input_gradient = grad_hidden + inverse1 * (scaled1 - unit1 * jnp.mean(scaled1 * unit1, axis=-1, keepdims=True))
    final = jnp.concatenate([late_piece, mixed[tok:].astype(BF16)], axis=0)
    final = to_all(jnp.broadcast_to(final[None], (groups,) + final.shape), "ctx")
    step = late_piece.shape[0]
    placed = place_slots(early_slots, tables, 12 * entries)
    late_sum = final[:, :step].reshape(columns, width).astype(F32)
    qkv_sum, out_sum = jnp.stack([late_sum, placed[0], placed[1]]).transpose(0, 2, 1), placed[2]
    small = jnp.sum(final[:, step:].astype(F32), axis=0).reshape(-1, quarter)
    table_sum = small[experts + 2, : buckets * heads].reshape(buckets, heads)
    return (output, input_gradient, small[experts], qkv_sum, table_sum, out_sum, small[experts + 1],
            small[:experts].T, grad_up_own, grad_down_own)


def solution(mesh):
    ctx, shard = mesh.shape["ctx"], mesh.shape["shard"]
    inner = jax.sharding.Mesh(mesh.devices.reshape(ctx, shard // 2, 2), ALL)
    ring = ring_of(ctx)
    tokens = P(ALL, None)
    in_specs = (tokens, P(SHARD), P(None, None, SHARD), P(None, SHARD), P(SHARD, None), P(SHARD), P(SHARD, None),
                P("ctx", None, SHARD), P("ctx", SHARD, None), tokens, tokens)
    out_specs = (tokens, tokens, P(SHARD), P(None, None, SHARD), P(None, SHARD), P(SHARD, None), P(SHARD),
                 P(SHARD, None), P("ctx", None, SHARD), P("ctx", SHARD, None))

    def step(layer_input, *args):
        half = 2 * layer_input.shape[0]
        return body(ring, entry_tables(ring, tile_count(ctx, half)), layer_input, *args)

    return jax.shard_map(step, mesh=inner, in_specs=in_specs, out_specs=out_specs, check_vma=False)
```
